32 devices in a mesh: freq: 16 (over z, x, core), lat: 2 (over y).
Axes of the slice: x: 2, y: 2, z: 4, core: 2. Of those that a mesh axis runs over, the one named last changes fastest.
Arguments:
- frequencies: float32 [16], P('freq'), may hold values from 0.3 to 1.5
- slowness: float32 [2, 32, 1024], P(None, 'lat', 'freq'), may hold values from 0.5 to 1.5
- src_field: float32 [16, 2, 32, 1024], P('freq', None, 'lat'), may hold values from -6 to 6
- rec_field: float32 [16, 2, 32, 1024], P('freq', None, 'lat'), may hold values from -6 to 6
Outputs:
- depth_image: float32 [2, 32, 1024], P(None, 'lat', 'freq')
- src_final: float32 [16, 2, 32, 1024], P('freq', None, 'lat')
- rec_final: float32 [16, 2, 32, 1024], P('freq', None, 'lat')
The draws below stay inside these ranges and needn't reach their ends.
All inputs are finite; a program needn't handle non-finite values.
Results may differ from the reference program's by a relative error of at most 0.0003.
Values sent between devices are 32-bit elements; how exact they have to be, the bound alone decides.
No kernel may reach another device: no remote copies, remote signals or barrier semaphores. Data moves between devices by JAX's collectives and lax.ppermute only.
A program may use at most 64 MiB of HBM per device.

```python
import math
import jax
import jax.numpy as jnp
from jax import lax

NY = 1024
NZ = 2
TERMS = 8
NW = 16
NX = 32


def level_of(rng, shape, split, smallest, largest):
    gain = 1.0
    for axis_at, blocks in split:
        draws = jax.random.uniform(jax.random.fold_in(jax.random.fold_in(rng, 6), axis_at), (blocks,), jnp.float32, smallest / len(split), largest / len(split))
        gain = gain * jnp.repeat(jnp.exp(draws), shape[axis_at] // blocks).reshape((-1,) + (1,) * (len(shape) - 1 - axis_at))
    return gain


def centred(stream_key, extent, deviation, most, pieces=(), kind=jnp.bfloat16):
    factor_of = level_of(stream_key, extent, pieces, -0.22, 0.18) if pieces else 1.0
    values = jax.random.normal(stream_key, extent, jnp.float32) * deviation * factor_of
    return jnp.minimum(jnp.maximum(values, -most), most).astype(kind)


def setup_inputs(seed: int = 0) -> dict:
    splits = jax.random.split(jax.random.key(seed), 5)
    return {
        "frequencies": jnp.clip(jnp.exp(math.log(1.5) - 1.60943787 * jax.random.uniform(splits[0], (NW,), jnp.float32) ** level_of(splits[0], (NW,), ((0, 16),), -0.2, 0.2)), 0.3, 1.5),
        "slowness": jnp.clip(jnp.exp(math.log(1.5) - 1.0986123 * jax.random.uniform(splits[1], (NZ, NX, NY), jnp.float32) ** level_of(splits[1], (NZ, NX, NY), ((1, 2), (2, 16)), -0.2, 0.2)), 0.5, 1.5),
        "src_field": centred(splits[2], (NW, 2, NX, NY), 1.0, 6.0, ((0, 16), (2, 2)), jnp.float32),
        "rec_field": centred(splits[3], (NW, 2, NX, NY), 1.0, 6.0, ((0, 16), (2, 2)), jnp.float32),
    }


step_ratio = 1.0
damping = 0.1

def neighbours(values):
    zero_col = jnp.zeros_like(values[..., :1])
    from_right = jnp.concatenate([values[..., 1:], zero_col], axis=-1)
    from_left = jnp.concatenate([zero_col, values[..., :-1]], axis=-1)
    return from_right + from_left

def mcclellan(padded):
    centre = padded[..., 1:-1, :]
    vertical = padded[..., 2:, :] + padded[..., :-2, :]
    return -0.5 * centre + 0.25 * vertical + neighbours(0.25 * centre + 0.125 * vertical)

def coefficients(wavenum, term_count):
    angles = math.pi * (jnp.arange(term_count, dtype=jnp.float32) + 0.5) / term_count
    view_shape = (term_count,) + (1,) * wavenum.ndim
    node_angles = angles.reshape(view_shape)
    excess = wavenum[None] ** 2 - node_angles ** 2
    absorb = damping * wavenum[None] ** 2
    modulus = jnp.sqrt(excess * excess + absorb * absorb)
    larger = jnp.sqrt(0.5 * (modulus + jnp.abs(excess)))
    smaller = absorb / (2.0 * larger)
    propagating = excess >= 0
    real_part = jnp.where(propagating, larger, smaller)
    imag_part = jnp.where(propagating, smaller, larger)
    attenuation = jnp.exp(-step_ratio * imag_part)
    phase_re = attenuation * jnp.cos(step_ratio * real_part)
    phase_im = attenuation * jnp.sin(step_ratio * real_part)
    orders = jnp.arange(term_count, dtype=jnp.float32)
    weights = jnp.where(orders == 0, 1.0, 2.0) / term_count
    cosine_table = (weights[:, None] * jnp.cos(orders[:, None] * angles[None, :])).astype(jnp.float32)
    coef_re = jnp.einsum('nj,j...->n...', cosine_table, phase_re, precision=lax.Precision.HIGHEST)
    coef_im = jnp.einsum('nj,j...->n...', cosine_table, phase_im, precision=lax.Precision.HIGHEST)
    return (coef_re, coef_im)

def accumulate(summed, coef_re, coef_im, level):
    src_re = level[..., 0, :, :]
    src_im = level[..., 1, :, :]
    rec_re = level[..., 2, :, :]
    rec_im = level[..., 3, :, :]
    term = jnp.stack([coef_re * src_re - coef_im * src_im, coef_re * src_im + coef_im * src_re, coef_re * rec_re + coef_im * rec_im, coef_re * rec_im - coef_im * rec_re], axis=-3)
    return summed + term

def pad_rows(values):
    widths = [(0, 0)] * (values.ndim - 2) + [(1, 1), (0, 0)]
    return jnp.pad(values, widths)

def reference(frequencies, slowness, src_field, rec_field):

    def one_frequency(inputs):
        frequency, source, receiver = inputs
        wavefields = jnp.concatenate([source, receiver], axis=0)
        images = []
        for depth_step in range(NZ):
            coef_re, coef_im = coefficients(frequency * slowness[depth_step], TERMS)
            previous = wavefields
            summed = accumulate(jnp.zeros_like(wavefields), coef_re[0], coef_im[0], previous)
            current = mcclellan(pad_rows(previous))
            summed = accumulate(summed, coef_re[1], coef_im[1], current)
            for term_index in range(2, TERMS):
                following = 2.0 * mcclellan(pad_rows(current)) - previous
                summed = accumulate(summed, coef_re[term_index], coef_im[term_index], following)
                previous, current = (current, following)
            wavefields = summed
            images.append(wavefields[0] * wavefields[2] + wavefields[1] * wavefields[3])
        return (wavefields, jnp.stack(images))
    wavefields, images = lax.map(one_frequency, (frequencies, src_field, rec_field))
    depth_image = lax.optimization_barrier(jnp.sum(images, axis=0)) * (1.0 / math.sqrt(NW))
    return (depth_image, wavefields[:, :2], wavefields[:, 2:])
```

```python
import functools
import math

import jax
import jax.numpy as jnp
from jax import lax
from jax.experimental import pallas as pl
from jax.experimental.pallas import tpu as pltpu
from jax.sharding import PartitionSpec as P

TERMS = 8
LANES = 128

damping = 0.1

SIN2 = (2.0, -0.3333333134651184, 0.01666657254099846, -0.0003966305812355131, 5.3452554311661515e-06)
COS = (1.0, -0.49999991059303284, 0.04166615381836891, -0.0013878209283575416, 2.3889762815088034e-05)


def horner(powers, x):
    total = powers[-1] * x + powers[-2]
    for power in powers[-3::-1]:
        total = total * x + power
    return total


def node_phases(wavenum):
    square = wavenum * wavenum
    absorb = damping * square
    absorb_square = absorb * absorb
    half_absorb = 0.5 * absorb
    phases = []
    for node in range(TERMS):
        angle = math.pi * (node + 0.5) / TERMS
        excess = square - angle * angle
        modulus_square = excess * excess + absorb_square
        modulus = modulus_square * lax.rsqrt(modulus_square)
        larger_square = 0.5 * (modulus + jnp.abs(excess))
        inverse = lax.rsqrt(larger_square)
        larger = larger_square * inverse
        smaller = half_absorb * inverse
        propagating = excess >= 0
        real_part = jnp.where(propagating, larger, smaller)
        imag_part = jnp.where(propagating, smaller, larger)
        attenuation = jnp.exp(-imag_part)
        half = 0.5 * real_part
        half_square = half * half
        sine2 = half * horner(SIN2, half_square)
        cosine = horner(COS, half_square)
        phases.append((attenuation * (1.0 - 0.5 * (sine2 * sine2)), attenuation * (sine2 * cosine)))
    return phases


def cosine_sums(values):
    half = TERMS // 2
    both = [values[j] + values[TERMS - 1 - j] for j in range(half)]
    apart = [values[j] - values[TERMS - 1 - j] for j in range(half)]
    outer, inner = both[0] + both[3], both[1] + both[2]
    outer_gap, inner_gap = both[0] - both[3], both[1] - both[2]
    scale = 2.0 / TERMS
    c1, c2, c3 = (scale * math.cos(math.pi * m / 8) for m in (1, 2, 3))
    sums = [None] * TERMS
    sums[0] = (1.0 / TERMS) * (outer + inner)
    sums[4] = c2 * (outer - inner)
    sums[2] = c1 * outer_gap + c3 * inner_gap
    sums[6] = c3 * outer_gap - c1 * inner_gap
    for order in range(1, TERMS, 2):
        row = [scale * math.cos(order * math.pi * (j + 0.5) / TERMS) for j in range(half)]
        sums[order] = (row[0] * apart[0] + row[1] * apart[1]) + (row[2] * apart[2] + row[3] * apart[3])
    return sums


def migrate_kernel(setup, place_ref, freq_ref, slow_ref, *refs):
    rows, tiles, depth_steps, two, packed, width = setup
    blocks = 2 if two else 3
    fields, refs = refs[: 2 * blocks], refs[2 * blocks :]
    image_ref, src_ref, rec_ref, levels, coefs = refs
    flip = place_ref[0]
    reach = TERMS - 1
    low_margin = 0 if two else reach
    lowest = -depth_steps * low_margin
    slow_rows = (blocks + depth_steps - 1) * rows if depth_steps > 1 else blocks * rows

    lane = lax.broadcasted_iota(jnp.int32, (tiles, LANES), 1)
    tile = lax.broadcasted_iota(jnp.int32, (tiles, LANES), 0)
    first_lane, last_lane = lane == 0, lane == LANES - 1
    first_tile, last_tile = tile == 0, tile == tiles - 1

    def spread(values):
        left = pltpu.roll(values, 1, 1)
        right = pltpu.roll(values, LANES - 1, 1)
        before = jnp.where(first_tile, 0.0, pltpu.roll(left, 1, 0))
        after = jnp.where(last_tile, 0.0, pltpu.roll(right, tiles - 1, 0))
        left = jnp.where(first_lane, before, left)
        right = jnp.where(last_lane, after, right)
        return (values + values) + (left + right)

    def strided(row):
        return (row // 8) * 8 * tiles + row % 8

    def local_start(row):
        if not two:
            return strided(row)
        here, there = strided(row), strided(rows - 1 - row)
        return here + flip * (there - here)

    def fetch(pair, part, row):
        if 0 <= row < rows:
            ref, start = fields[pair * blocks], local_start(row)
        elif two:
            here, there = strided(row - rows), strided(2 * rows - 1 - row)
            ref, start = fields[pair * blocks + 1], here + flip * (there - here)
        elif row < 0:
            ref, start = fields[pair * blocks + 1], strided(rows + row)
        else:
            ref, start = fields[pair * blocks + 2], strided(row - rows)
        return ref[part, pl.ds(start, tiles, stride=8), :]

    for pair in range(2):
        for row in range(lowest, rows + depth_steps * reach):
            real, imag = fetch(pair, 0, row), fetch(pair, 1, row)
            levels[0, 2 * pair, row - lowest] = real
            levels[0, 2 * pair + 1, row - lowest] = -imag if pair else imag

    images = []
    for step in range(depth_steps):
        later = depth_steps - 1 - step
        low, high = -low_margin * later, rows + reach * later

        def slow_row(row, step=step):
            own = row if not two else row + flip * (rows - 1 - 2 * row)
            if step:
                return (blocks + step - 1) * rows + own
            if two:
                other = row + flip * (3 * rows - 1 - 2 * row)
                return jnp.where(row < rows, own, other)
            return jnp.where(row < 0, 2 * rows + row, jnp.where(row < rows, row, row + rows))

        def coefficient_row(row, carry, step=step):
            slow = slow_ref[pl.ds(slow_row(row), tiles, stride=slow_rows), :]
            phases = node_phases(freq_ref[0] * slow)
            for part in range(2):
                for order, value in enumerate(cosine_sums([p[part] for p in phases])):
                    coefs[order, part, row - lowest] = value
            return carry

        lax.fori_loop(low, high, coefficient_row, 0)

        def chebyshev(field, carry, low=low, high=high):
            for order in range(1, TERMS):
                left = TERMS - 1 - order
                begin = low if two else low - left
                end = high + left
                above = None if two else spread(levels[order - 1, field, begin - 1 - lowest])
                here = spread(levels[order - 1, field, begin - lowest])
                for row in range(begin, end):
                    below = spread(levels[order - 1, field, row + 1 - lowest])
                    total = here + here + below
                    if above is not None:
                        total = total + above
                    centre = levels[order - 1, field, row - lowest]
                    if order == 1:
                        value = 0.125 * total - centre
                    else:
                        value = (0.25 * total - (centre + centre)) - levels[order - 2, field, row - lowest]
                    if not two and row < 0:
                        value = value * place_ref[1].astype(jnp.float32)
                    if not two and row >= rows:
                        value = value * place_ref[2].astype(jnp.float32)
                    levels[order, field, row - lowest] = value
                    above, here = here, below
            return carry

        lax.fori_loop(0, 4, chebyshev, 0)

        row_images = []
        for row in range(low, high):
            at = row - lowest
            outs = []
            for pair in range(2):
                real = imag = None
                for order in range(TERMS):
                    coef_re, coef_im = coefs[order, 0, at], coefs[order, 1, at]
                    field_re, field_im = levels[order, 2 * pair, at], levels[order, 2 * pair + 1, at]
                    term_re = coef_re * field_re - coef_im * field_im
                    term_im = coef_re * field_im + coef_im * field_re
                    real = term_re if real is None else real + term_re
                    imag = term_im if imag is None else imag + term_im
                outs += [real, imag]
            if later:
                for field in range(4):
                    levels[0, field, at] = outs[field]
            else:
                start = local_start(row)
                src_ref[0, pl.ds(start, tiles, stride=8), :] = outs[0]
                src_ref[1, pl.ds(start, tiles, stride=8), :] = outs[1]
                rec_ref[0, pl.ds(start, tiles, stride=8), :] = outs[2]
                rec_ref[1, pl.ds(start, tiles, stride=8), :] = -outs[3]
            if 0 <= row < rows:
                value = outs[0] * outs[2] - outs[1] * outs[3]
                if not packed:
                    image_ref[step, pl.ds(local_start(row), tiles, stride=8), :] = value
                elif not later:
                    first = images[0][row]
                    own = row if not two else row + flip * (rows - 1 - 2 * row)
                    in_low = lane < width
                    even = jnp.where(in_low, first, pltpu.roll(value, width, 1))
                    odd = jnp.where(in_low, pltpu.roll(first, width, 1), value)
                    image_ref[pl.ds(own, tiles, stride=2 * rows), :] = even
                    image_ref[pl.ds(rows + own, tiles, stride=2 * rows), :] = odd
                row_images.append(value)
        images.append(row_images)


def tiled(block):
    parts, rows, columns = block.shape
    split = block.reshape(parts, rows // 8, 8, columns // LANES, LANES)
    return split.transpose(0, 1, 3, 2, 4).reshape(parts, rows * columns // LANES, LANES)


def untiled(block, rows):
    parts, count, _ = block.shape
    tiles = count // rows
    split = block.reshape(parts, rows // 8, tiles, 8, LANES)
    return split.transpose(0, 1, 3, 2, 4).reshape(parts, rows, tiles * LANES)


def from_side(block, side):
    count = lax.axis_size("lat")
    links = [(i, i - side) for i in range(count) if 0 <= i - side < count]
    return lax.ppermute(block, "lat", links)


def from_sides(block):
    if lax.axis_size("lat") == 2:
        return [lax.ppermute(block, "lat", [(0, 1), (1, 0)])]
    return [from_side(block, -1), from_side(block, 1)]


def gather_columns(block):
    count = lax.axis_size("freq")
    me = lax.axis_index("freq")
    rows, width = block.shape
    bits = [1 << i for i in range(count.bit_length() - 1)]
    inner = [b for b in bits if b * width < LANES]
    outer = [b for b in bits if b * width >= LANES][::-1]

    def partner(held, bit):
        return lax.ppermute(held, "freq", [(i, i ^ bit) for i in range(count)])

    for bit in inner:
        other = partner(block, bit)
        upper = (me & bit) != 0
        block = jnp.concatenate([jnp.where(upper, other, block), jnp.where(upper, block, other)], axis=1)
    for depth, bit in enumerate(outer):
        other = partner(block, bit)
        upper = (me & bit) != 0
        block = jnp.stack([jnp.where(upper, other, block), jnp.where(upper, block, other)], axis=depth)
    return block.reshape((count * width // LANES) * rows, LANES)


def shards(frequencies, slowness, src_field, rec_field):
    depth_steps, rows, width = slowness.shape
    columns = src_field.shape[3]
    tiles = columns // LANES
    freq_count = lax.axis_size("freq")
    lat_count = lax.axis_size("lat")
    lat_index = lax.axis_index("lat")
    two = lat_count == 2
    packed = depth_steps == 2 and width * depth_steps == LANES
    norm_factor = 1.0 / math.sqrt(frequencies.shape[0] * freq_count)

    slow_sides = from_sides(slowness[0])
    src_sides, rec_sides = from_sides(src_field[0]), from_sides(rec_field[0])
    if two:
        slow_parts = [slowness[0], slow_sides[0]]
    else:
        slow_parts = [slowness[0], slow_sides[0], slow_sides[1]]
    slow_parts += [slowness[z] for z in range(1, depth_steps)]
    slow = gather_columns(jnp.concatenate(slow_parts, axis=0))

    place = jnp.stack(
        [lat_index if two else 0, (lat_index > 0).astype(jnp.int32), (lat_index < lat_count - 1).astype(jnp.int32)]
    ).astype(jnp.int32)
    fields = [tiled(x) for x in (src_field[0], *src_sides, rec_field[0], *rec_sides)]
    reach = TERMS - 1
    span = rows + depth_steps * reach * (1 if two else 2)
    image_shape = (freq_count * rows, LANES) if packed else (depth_steps, rows * tiles, LANES)
    field_shape = jax.ShapeDtypeStruct((2, rows * tiles, LANES), jnp.float32)
    setup = (rows, tiles, depth_steps, two, packed, width)
    image, src, rec = pl.pallas_call(
        functools.partial(migrate_kernel, setup),
        out_shape=(jax.ShapeDtypeStruct(image_shape, jnp.float32), field_shape, field_shape),
        in_specs=[pl.BlockSpec(memory_space=pltpu.SMEM)] * 2
        + [pl.BlockSpec(memory_space=pltpu.VMEM)] * (1 + len(fields)),
        out_specs=(pl.BlockSpec(memory_space=pltpu.VMEM),) * 3,
        scratch_shapes=[
            pltpu.VMEM((TERMS, 4, span, tiles, LANES), jnp.float32),
            pltpu.VMEM((TERMS, 2, span, tiles, LANES), jnp.float32),
        ],
        name="migrate",
    )(place, frequencies, slow, *fields)

    if packed:
        pieces = image.reshape(freq_count, rows, LANES)
        total = jnp.sum(lax.all_to_all(pieces, "freq", 0, 0, tiled=True), axis=0) * norm_factor
        depth_image = jnp.stack([total[:, z * width : (z + 1) * width] for z in range(depth_steps)])
    else:
        whole = untiled(image, rows).reshape(depth_steps, rows, freq_count, width)
        pieces = whole.transpose(2, 0, 1, 3)
        depth_image = jnp.sum(lax.all_to_all(pieces, "freq", 0, 0, tiled=True), axis=0) * norm_factor
    return (depth_image, untiled(src, rows)[None], untiled(rec, rows)[None])


def solution(mesh):
    placed = (
        P("freq"),
        P(None, "lat", "freq"),
        P("freq", None, "lat", None),
        P("freq", None, "lat", None),
    )
    return jax.shard_map(
        shards,
        mesh=mesh,
        in_specs=placed,
        out_specs=(
            P(None, "lat", "freq"),
            P("freq", None, "lat", None),
            P("freq", None, "lat", None),
        ),
        check_vma=False,
    )
```

```python
import functools
import math

import jax
import jax.numpy as jnp
from jax import lax
from jax.experimental import pallas as pl
from jax.experimental.pallas import tpu as pltpu
from jax.sharding import PartitionSpec as P

TERMS = 8
REACH = TERMS - 1
LANES = 128
SUBLANES = 8

damping = 0.1

SINE = (0.5, -0.010416666045784950, 6.510379898820e-05, -1.9366727e-07, 3.26248263e-10)


def horner(powers, x):
    total = powers[-1] * x + powers[-2]
    for power in powers[-3::-1]:
        total = total * x + power
    return total


def node_phases(wavenum):
    square = wavenum * wavenum
    absorb = damping * square
    absorb_square = absorb * absorb
    phases = []
    for node in range(TERMS):
        angle = math.pi * (node + 0.5) / TERMS
        excess = square - angle * angle
        modulus_square = excess * excess + absorb_square
        doubled = modulus_square * lax.rsqrt(modulus_square) + jnp.abs(excess)
        inverse = lax.rsqrt(doubled)
        larger = doubled * inverse
        smaller = absorb * inverse
        propagating = excess >= 0
        real_part = jnp.where(propagating, larger, smaller)
        imag_part = jnp.where(propagating, smaller, larger)
        attenuation = jnp.exp(imag_part * -math.sqrt(0.5))
        sine = real_part * horner(SINE, real_part * real_part)
        sine_square = sine * sine
        rest = 2.0 - sine_square
        phase_re = attenuation * (1.0 - sine_square)
        phase_im = attenuation * (sine * (rest * lax.rsqrt(rest)))
        phases.append((phase_re, phase_im))
    return phases


def cosine_sums(values):
    half = TERMS // 2
    both = [values[j] + values[TERMS - 1 - j] for j in range(half)]
    apart = [values[j] - values[TERMS - 1 - j] for j in range(half)]
    outer, inner = both[0] + both[3], both[1] + both[2]
    outer_gap, inner_gap = both[0] - both[3], both[1] - both[2]
    scale = 2.0 / TERMS
    c1, c2, c3 = (scale * math.cos(math.pi * m / 8) for m in (1, 2, 3))
    sums = [None] * TERMS
    sums[0] = (1.0 / TERMS) * (outer + inner)
    sums[4] = c2 * (outer - inner)
    sums[2] = c1 * outer_gap + c3 * inner_gap
    sums[6] = c3 * outer_gap - c1 * inner_gap
    for order in range(1, TERMS, 2):
        row = [scale * math.cos(order * math.pi * (j + 0.5) / TERMS) for j in range(half)]
        sums[order] = (row[0] * apart[0] + row[1] * apart[1]) + (row[2] * apart[2] + row[3] * apart[3])
    return sums


def window(rows, later, two):
    return (0 if two else -REACH * later), rows + REACH * later


def strided(row, tiles):
    return (row // SUBLANES) * SUBLANES * tiles + row % SUBLANES


def either(flip, here, there):
    return here + flip * (there - here)


def spreader(tiles):
    lane = lax.broadcasted_iota(jnp.int32, (tiles, LANES), 1)
    tile = lax.broadcasted_iota(jnp.int32, (tiles, LANES), 0)
    first_lane, last_lane = lane == 0, lane == LANES - 1
    first_tile, last_tile = tile == 0, tile == tiles - 1

    def spread(values):
        left = pltpu.roll(values, 1, 1)
        right = pltpu.roll(values, LANES - 1, 1)
        before = jnp.where(first_tile, 0.0, pltpu.roll(left, 1, 0))
        after = jnp.where(last_tile, 0.0, pltpu.roll(right, tiles - 1, 0))
        left = jnp.where(first_lane, before, left)
        right = jnp.where(last_lane, after, right)
        return (values + values) + (left + right)

    return spread


def chebyshev(levels, fields, low, high, lowest, rows, two):
    spread = spreader(levels.shape[3])
    if not two:
        lat = lax.axis_index("lat")
        inside_low = (lat > 0).astype(jnp.float32)
        inside_high = (lat < lax.axis_size("lat") - 1).astype(jnp.float32)
    for order in range(1, TERMS):
        left = TERMS - 1 - order
        begin, end = (low if two else low - left), high + left
        above = [None if two else spread(levels[order - 1, f, begin - 1 - lowest]) for f in fields]
        here = [spread(levels[order - 1, f, begin - lowest]) for f in fields]
        for row in range(begin, end):
            for k, f in enumerate(fields):
                below = spread(levels[order - 1, f, row + 1 - lowest])
                total = (here[k] + here[k]) + below
                if above[k] is not None:
                    total = total + above[k]
                centre = levels[order - 1, f, row - lowest]
                if order == 1:
                    value = 0.125 * total - centre
                else:
                    value = (0.25 * total - (centre + centre)) - levels[order - 2, f, row - lowest]
                if not two and row < 0:
                    value = value * inside_low
                if not two and row >= rows:
                    value = value * inside_high
                levels[order, f, row - lowest] = value
                above[k], here[k] = here[k], below


def first_kernel(rows, depth_steps, two, conjugate, *refs):
    fields, levels = refs[:-1], refs[-1]
    tiles = levels.shape[3]
    flip = lax.axis_index("lat")
    low, high = window(rows, depth_steps - 1, two)
    lowest = low if two else low - REACH
    for row in range(lowest, high + REACH):
        if two:
            side = 0 if row < rows else 1
            ref, near = fields[side], row - side * rows
            start = either(flip, strided(near, tiles), strided(rows - 1 - near, tiles))
        else:
            side = 1 if row < 0 else 2 if row >= rows else 0
            ref, start = fields[side], strided(row + (0, rows, -rows)[side], tiles)
        for part in range(2):
            value = ref[part, pl.ds(start, tiles, stride=SUBLANES), :]
            levels[0, part, row - lowest] = -value if part and conjugate else value
    chebyshev(levels, (0, 1), low, high, lowest, rows, two)


def coefficient_kernel(bit, other, *refs):
    freq_ref, slow_ref, out_ref = refs[0], refs[1], refs[-1]
    count, rows, _ = slow_ref.shape
    slot = (lax.axis_index("freq") >> bit) & 1
    if other:
        slot = 1 - slot
    groups = rows // SUBLANES

    def body(index, carry):
        piece = index // groups
        start = pl.multiple_of((index % groups) * SUBLANES, SUBLANES)
        phases = node_phases(freq_ref[0] * slow_ref[piece, pl.ds(start, SUBLANES), :])
        for part in range(2):
            for order, value in enumerate(cosine_sums([p[part] for p in phases])):
                out_ref[order, part, 2 * piece + slot, pl.ds(start, SUBLANES), :] = value
        return carry

    lax.fori_loop(0, count * groups, body, 0)


def main_kernel(setup, coef_ref, src_levels, rec_levels, *refs):
    rows, halo, depth_steps, two, packed, width = setup
    image_refs, (src_ref, rec_ref, levels) = refs[:-3], refs[-3:]
    tiles = levels.shape[3]
    coef_rows = coef_ref.shape[2] // tiles
    flip = lax.axis_index("lat")
    lane = lax.broadcasted_iota(jnp.int32, (tiles, LANES), 1)
    tile = lax.broadcasted_iota(jnp.int32, (tiles, LANES), 0)
    in_low = lane < width
    if packed:
        parity, me, count = tile * 0, lax.axis_index("freq"), lax.axis_size("freq")
        for bit in range(count.bit_length() - 1):
            parity = parity ^ (tile >> bit) ^ (me >> bit)
        keeps_even = (parity & 1) == 0

    def own(row):
        return either(flip, row, rows - 1 - row) if two else row

    def own_start(row):
        return either(flip, strided(row, tiles), strided(rows - 1 - row, tiles)) if two else strided(row, tiles)

    def coef_row(step, row):
        sides = 1 if two else 2
        if step:
            return rows + sides * halo + (step - 1) * rows + own(row)
        if 0 <= row < rows:
            return own(row)
        if two:
            return rows + either(flip, row - rows, halo - 1 - (row - rows))
        return rows + halo + (row if row < 0 else row - rows)

    images = []
    for step in range(depth_steps):
        later = depth_steps - 1 - step
        low, high = window(rows, later, two)
        lowest = window(rows, max(later, 1), two)[0]
        if step:

            def pair_fields(pair, carry, low=low, high=high, lowest=lowest):
                chebyshev(levels, (2 * pair, 2 * pair + 1), low, high, lowest, rows, two)
                return carry

            lax.fori_loop(0, 2, pair_fields, 0)
        top = low if two else low - REACH
        next_lowest = window(rows, max(later - 1, 1), two)[0]
        row_images = []
        for row in range(low, high):
            start = coef_row(step, row)
            coefs = [
                [coef_ref[order, part, pl.ds(start, tiles, stride=coef_rows), :] for part in range(2)]
                for order in range(TERMS)
            ]
            outs = []
            for pair in range(2):
                real = imag = None
                for order, (coef_re, coef_im) in enumerate(coefs):
                    if step:
                        field_re = levels[order, 2 * pair, row - lowest]
                        field_im = levels[order, 2 * pair + 1, row - lowest]
                    else:
                        source = rec_levels if pair else src_levels
                        field_re, field_im = source[order, 0, row - top], source[order, 1, row - top]
                    term_re = coef_re * field_re - coef_im * field_im
                    term_im = coef_re * field_im + coef_im * field_re
                    real = term_re if real is None else real + term_re
                    imag = term_im if imag is None else imag + term_im
                outs += [real, imag]
            if later:
                for field in range(4):
                    levels[0, field, row - next_lowest] = outs[field]
            else:
                at = pl.ds(own_start(row), tiles, stride=SUBLANES)
                src_ref[0, at, :] = outs[0]
                src_ref[1, at, :] = outs[1]
                rec_ref[0, at, :] = outs[2]
                rec_ref[1, at, :] = -outs[3]
            if not 0 <= row < rows:
                continue
            value = outs[0] * outs[2] - outs[1] * outs[3]
            row_images.append(value)
            if not packed:
                image_refs[0][step, pl.ds(own_start(row), tiles, stride=SUBLANES), :] = value
            elif not later:
                first = images[0][row]
                even = jnp.where(in_low, first, pltpu.roll(value, width, 1))
                odd = jnp.where(in_low, pltpu.roll(first, width, 1), value)
                at = pl.ds(own(row), tiles, stride=rows)
                image_refs[0][at, :] = jnp.where(keeps_even, even, odd)
                image_refs[1][at, :] = jnp.where(keeps_even, odd, even)
        images.append(row_images)


def tiled(block):
    parts, rows, columns = block.shape
    split = block.reshape(parts, rows // SUBLANES, SUBLANES, columns // LANES, LANES)
    return split.transpose(0, 1, 3, 2, 4).reshape(parts, rows * columns // LANES, LANES)


def untiled(block, rows):
    parts, count, _ = block.shape
    tiles = count // rows
    split = block.reshape(parts, rows // SUBLANES, tiles, SUBLANES, LANES)
    return split.transpose(0, 1, 3, 2, 4).reshape(parts, rows, tiles * LANES)


def from_sides(block):
    count = lax.axis_size("lat")
    if count == 2:
        return [lax.ppermute(block, "lat", [(0, 1), (1, 0)])]
    return [
        lax.ppermute(block, "lat", [(i, i - side) for i in range(count) if 0 <= i - side < count]) for side in (-1, 1)
    ]


def partner(block, mask):
    return lax.ppermute(block, "freq", [(i, i ^ mask) for i in range(lax.axis_size("freq"))])


def gather_columns(block):
    count = lax.axis_size("freq")
    me = lax.axis_index("freq")
    width = block.shape[1]
    bits = range(count.bit_length() - 1)
    inner = [b for b in bits if width << b < LANES]
    outer = [b for b in bits if width << b >= LANES][::-1]
    for b in inner:
        other = partner(block, 1 << b)
        upper = (me >> b) & 1 != 0
        block = jnp.concatenate([jnp.where(upper, other, block), jnp.where(upper, block, other)], axis=1)
    block = block[None]
    for depth, b in enumerate(outer):
        other = partner(block, (1 << b) | (1 if inner else 0))
        if b == outer[-1]:
            return block, other, b
        upper = (me >> b) & 1 != 0
        low, high = jnp.where(upper, other, block), jnp.where(upper, block, other)
        block = jnp.stack([low, high], axis=1).reshape(2 * block.shape[0], *block.shape[1:])


def scatter_sum(keep, send, rows):
    count = lax.axis_size("freq")
    me = lax.axis_index("freq")
    held = (keep + partner(send, 1)).reshape(count // 2, rows, LANES)
    for b in range(1, count.bit_length() - 1):
        upper = (me >> b) & 1 != 0
        split = held.reshape(held.shape[0] // 2, 2, rows, LANES)
        low, high = split[:, 0], split[:, 1]
        held = jnp.where(upper, high, low) + partner(jnp.where(upper, low, high), (1 << b) | 1)
    return held[0]


def shards(frequencies, slowness, src_field, rec_field):
    depth_steps, rows, width = slowness.shape
    tiles = src_field.shape[3] // LANES
    freq_count = lax.axis_size("freq")
    flip = lax.axis_index("lat")
    two = lax.axis_size("lat") == 2
    packed = depth_steps == 2 and width * depth_steps == LANES
    norm_factor = 1.0 / math.sqrt(frequencies.shape[0] * freq_count)
    halo = -(-REACH * (depth_steps - 1) // SUBLANES) * SUBLANES
    low, high = window(rows, depth_steps - 1, two)
    span = high + REACH - (low if two else low - REACH)
    later_span = window(rows, 1, two)[1] - window(rows, 1, two)[0]

    slow_sides = from_sides(slowness)
    src_sides, rec_sides = from_sides(src_field), from_sides(rec_field)
    slow_parts = [slowness[0]]
    if two:
        slow_parts.append(jnp.where(flip == 0, slow_sides[0][0, :halo], slow_sides[0][0, rows - halo :]))
    else:
        slow_parts += [slow_sides[0][0, rows - halo :], slow_sides[1][0, :halo]]
    slow_parts += [slowness[z] for z in range(1, depth_steps)]
    mine, theirs, bit = gather_columns(jnp.concatenate(slow_parts, axis=0))
    coef_rows = mine.shape[1]

    smem, vmem = pl.BlockSpec(memory_space=pltpu.SMEM), pl.BlockSpec(memory_space=pltpu.VMEM)
    shape_of = functools.partial(jax.ShapeDtypeStruct, dtype=jnp.float32)

    def limit(mib):
        return pltpu.CompilerParams(vmem_limit_bytes=mib << 20)

    def first_levels(own, sides, conjugate):
        fields = [tiled(x[0]) for x in (own, *sides)]
        return pl.pallas_call(
            functools.partial(first_kernel, rows, depth_steps, two, conjugate),
            out_shape=shape_of((TERMS, 2, span, tiles, LANES)),
            in_specs=[vmem] * len(fields),
            out_specs=vmem,
            compiler_params=limit(4),
            cost_estimate=pl.CostEstimate(flops=1 << 26, bytes_accessed=1 << 22, transcendentals=0),
            name="first",
        )(*fields)

    src_levels = first_levels(src_field, src_sides, False)
    rec_levels = first_levels(rec_field, rec_sides, True)

    coef_shape = shape_of((TERMS, 2, tiles, coef_rows, LANES))

    def coefficients(other, *operands):
        return pl.pallas_call(
            functools.partial(coefficient_kernel, bit, other),
            out_shape=coef_shape,
            in_specs=[smem] + [vmem] * (len(operands) - 1),
            out_specs=vmem,
            input_output_aliases={2: 0} if other else {},
            compiler_params=limit(8),
            cost_estimate=pl.CostEstimate(flops=1 << 26, bytes_accessed=1 << 22, transcendentals=0),
            name="coefficients",
        )(*operands)

    coefs = coefficients(False, frequencies, mine)
    coefs = coefficients(True, frequencies, theirs, coefs)

    image_shape = shape_of((tiles * rows, LANES) if packed else (depth_steps, rows * tiles, LANES))
    field_shape = shape_of((2, rows * tiles, LANES))
    image_shapes = [image_shape] * (2 if packed else 1)
    setup = (rows, halo, depth_steps, two, packed, width)
    *image, src, rec = pl.pallas_call(
        functools.partial(main_kernel, setup),
        out_shape=(*image_shapes, field_shape, field_shape),
        in_specs=[vmem] * 3,
        out_specs=(vmem,) * (len(image_shapes) + 2),
        scratch_shapes=[pltpu.VMEM((TERMS, 4, later_span, tiles, LANES), jnp.float32)],
        compiler_params=limit(16),
        name="main",
    )(coefs.reshape(TERMS, 2, tiles * coef_rows, LANES), src_levels, rec_levels)

    if packed:
        total = scatter_sum(*image, rows) * norm_factor
        depth_image = jnp.stack([total[:, z * width : (z + 1) * width] for z in range(depth_steps)])
    else:
        whole = untiled(image[0], rows).reshape(depth_steps, rows, freq_count, width)
        pieces = whole.transpose(2, 0, 1, 3)
        depth_image = jnp.sum(lax.all_to_all(pieces, "freq", 0, 0, tiled=True), axis=0) * norm_factor
    return (depth_image, untiled(src, rows)[None], untiled(rec, rows)[None])


def solution(mesh):
    placed = (
        P("freq"),
        P(None, "lat", "freq"),
        P("freq", None, "lat", None),
        P("freq", None, "lat", None),
    )
    return jax.shard_map(
        shards,
        mesh=mesh,
        in_specs=placed,
        out_specs=(
            P(None, "lat", "freq"),
            P("freq", None, "lat", None),
            P("freq", None, "lat", None),
        ),
        check_vma=False,
    )
```

```python
import functools
import math

import jax
import jax.numpy as jnp
from jax import lax
from jax.experimental import pallas as pl
from jax.experimental.pallas import tpu as pltpu
from jax.sharding import PartitionSpec as P

TERMS = 8
REACH = TERMS - 1
LANES = 128
SUBLANES = 8

damping = 0.1

SINE = (0.5, -0.010416666045784950, 6.510379898820e-05, -1.9366727e-07, 3.26248263e-10)


def horner(powers, x):
    total = powers[-1] * x + powers[-2]
    for power in powers[-3::-1]:
        total = total * x + power
    return total


def node_phases(wavenum):
    square = wavenum * wavenum
    absorb = damping * square
    absorb_square = absorb * absorb
    phases = []
    for node in range(TERMS):
        angle = math.pi * (node + 0.5) / TERMS
        excess = square - angle * angle
        modulus_square = excess * excess + absorb_square
        doubled = modulus_square * lax.rsqrt(modulus_square) + jnp.abs(excess)
        inverse = lax.rsqrt(doubled)
        larger = doubled * inverse
        smaller = absorb * inverse
        propagating = excess >= 0
        real_part = jnp.where(propagating, larger, smaller)
        imag_part = jnp.where(propagating, smaller, larger)
        attenuation = jnp.exp(imag_part * -math.sqrt(0.5))
        sine = real_part * horner(SINE, real_part * real_part)
        sine_square = sine * sine
        rest = 2.0 - sine_square
        phase_re = attenuation * (1.0 - sine_square)
        phase_im = attenuation * (sine * (rest * lax.rsqrt(rest)))
        phases.append((phase_re, phase_im))
    return phases


def cosine_sums(values):
    half = TERMS // 2
    both = [values[j] + values[TERMS - 1 - j] for j in range(half)]
    apart = [values[j] - values[TERMS - 1 - j] for j in range(half)]
    outer, inner = both[0] + both[3], both[1] + both[2]
    outer_gap, inner_gap = both[0] - both[3], both[1] - both[2]
    scale = 2.0 / TERMS
    c1, c2, c3 = (scale * math.cos(math.pi * m / 8) for m in (1, 2, 3))
    sums = [None] * TERMS
    sums[0] = (1.0 / TERMS) * (outer + inner)
    sums[4] = c2 * (outer - inner)
    sums[2] = c1 * outer_gap + c3 * inner_gap
    sums[6] = c3 * outer_gap - c1 * inner_gap
    for order in range(1, TERMS, 2):
        row = [scale * math.cos(order * math.pi * (j + 0.5) / TERMS) for j in range(half)]
        sums[order] = (row[0] * apart[0] + row[1] * apart[1]) + (row[2] * apart[2] + row[3] * apart[3])
    return sums


def window(rows, later, two):
    return (0 if two else -REACH * later), rows + REACH * later


def strided(row, tiles):
    return (row // SUBLANES) * SUBLANES * tiles + row % SUBLANES


def either(flip, here, there):
    return here + flip * (there - here)


def spreader(tiles):
    lane = lax.broadcasted_iota(jnp.int32, (tiles, LANES), 1)
    tile = lax.broadcasted_iota(jnp.int32, (tiles, LANES), 0)
    first_lane, last_lane = lane == 0, lane == LANES - 1
    first_tile, last_tile = tile == 0, tile == tiles - 1

    def spread(values):
        left = pltpu.roll(values, 1, 1)
        right = pltpu.roll(values, LANES - 1, 1)
        before = jnp.where(first_tile, 0.0, pltpu.roll(left, 1, 0))
        after = jnp.where(last_tile, 0.0, pltpu.roll(right, tiles - 1, 0))
        left = jnp.where(first_lane, before, left)
        right = jnp.where(last_lane, after, right)
        return (values + values) + (left + right)

    return spread


def chebyshev(levels, fields, low, high, lowest, rows, two):
    spread = spreader(levels.shape[3])
    if not two:
        lat = lax.axis_index("lat")
        inside_low = (lat > 0).astype(jnp.float32)
        inside_high = (lat < lax.axis_size("lat") - 1).astype(jnp.float32)
    for order in range(1, TERMS):
        left = TERMS - 1 - order
        begin, end = (low if two else low - left), high + left
        above = [None if two else spread(levels[order - 1, f, begin - 1 - lowest]) for f in fields]
        here = [spread(levels[order - 1, f, begin - lowest]) for f in fields]
        for row in range(begin, end):
            for k, f in enumerate(fields):
                below = spread(levels[order - 1, f, row + 1 - lowest])
                total = (here[k] + here[k]) + below
                if above[k] is not None:
                    total = total + above[k]
                centre = levels[order - 1, f, row - lowest]
                if order == 1:
                    value = 0.125 * total - centre
                else:
                    value = (0.25 * total - (centre + centre)) - levels[order - 2, f, row - lowest]
                if not two and row < 0:
                    value = value * inside_low
                if not two and row >= rows:
                    value = value * inside_high
                levels[order, f, row - lowest] = value
                above[k], here[k] = here[k], below


def first_kernel(rows, depth_steps, two, conjugate, *refs):
    fields, levels = refs[:-1], refs[-1]
    tiles = levels.shape[3]
    flip = lax.axis_index("lat")
    low, high = window(rows, depth_steps - 1, two)
    lowest = low if two else low - REACH
    for row in range(lowest, high + REACH):
        if two:
            side = 0 if row < rows else 1
            ref, near = fields[side], row - side * rows
            start = either(flip, strided(near, tiles), strided(rows - 1 - near, tiles))
        else:
            side = 1 if row < 0 else 2 if row >= rows else 0
            ref, start = fields[side], strided(row + (0, rows, -rows)[side], tiles)
        for part in range(2):
            value = ref[part, pl.ds(start, tiles, stride=SUBLANES), :]
            levels[0, part, row - lowest] = -value if part and conjugate else value
    chebyshev(levels, (0, 1), low, high, lowest, rows, two)


def coefficient_kernel(shared, *refs):
    freq_ref, slow_ref, out_ref = refs[0], refs[1], refs[-1]
    count, rows, _ = slow_ref.shape
    slot = 0
    for bit, other in shared:
        own = (lax.axis_index("freq") >> bit) & 1
        slot = 2 * slot + (1 - own if other else own)
    groups = rows // SUBLANES
    freq = jnp.broadcast_to(freq_ref[...], (SUBLANES, LANES))

    def body(index, carry):
        piece = index // groups
        start = pl.multiple_of((index % groups) * SUBLANES, SUBLANES)
        phases = node_phases(freq * slow_ref[piece, pl.ds(start, SUBLANES), :])
        for part in range(2):
            for order, value in enumerate(cosine_sums([p[part] for p in phases])):
                out_ref[order, part, (piece << len(shared)) + slot, pl.ds(start, SUBLANES), :] = value
        return carry

    lax.fori_loop(0, count * groups, body, 0)


def main_kernel(setup, coef_ref, src_levels, rec_levels, *refs):
    rows, halo, depth_steps, two, packed, width = setup
    image_refs, (src_ref, rec_ref, levels) = refs[:-3], refs[-3:]
    tiles = levels.shape[3]
    coef_rows = coef_ref.shape[2] // tiles
    flip = lax.axis_index("lat")
    lane = lax.broadcasted_iota(jnp.int32, (tiles, LANES), 1)
    tile = lax.broadcasted_iota(jnp.int32, (tiles, LANES), 0)
    in_low = lane < width
    if packed:
        parity, me, count = tile * 0, lax.axis_index("freq"), lax.axis_size("freq")
        for bit in range(count.bit_length() - 1):
            parity = parity ^ (tile >> bit) ^ (me >> bit)
        keeps_even = (parity & 1) == 0

    def own(row):
        return either(flip, row, rows - 1 - row) if two else row

    def own_start(row):
        return either(flip, strided(row, tiles), strided(rows - 1 - row, tiles)) if two else strided(row, tiles)

    def coef_row(step, row):
        sides = 1 if two else 2
        if step:
            return rows + sides * halo + (step - 1) * rows + own(row)
        if 0 <= row < rows:
            return own(row)
        if two:
            return rows + either(flip, row - rows, halo - 1 - (row - rows))
        return rows + halo + (row if row < 0 else row - rows)

    images = []
    for step in range(depth_steps):
        later = depth_steps - 1 - step
        low, high = window(rows, later, two)
        lowest = window(rows, max(later, 1), two)[0]
        if step:

            def pair_fields(pair, carry, low=low, high=high, lowest=lowest):
                chebyshev(levels, (2 * pair, 2 * pair + 1), low, high, lowest, rows, two)
                return carry

            lax.fori_loop(0, 2, pair_fields, 0)
        top = low if two else low - REACH
        next_lowest = window(rows, max(later - 1, 1), two)[0]
        row_images = []
        for row in range(low, high):
            start = coef_row(step, row)
            coefs = [
                [coef_ref[order, part, pl.ds(start, tiles, stride=coef_rows), :] for part in range(2)]
                for order in range(TERMS)
            ]
            outs = []
            for pair in range(2):
                real = imag = None
                for order, (coef_re, coef_im) in enumerate(coefs):
                    if step:
                        field_re = levels[order, 2 * pair, row - lowest]
                        field_im = levels[order, 2 * pair + 1, row - lowest]
                    else:
                        source = rec_levels if pair else src_levels
                        field_re, field_im = source[order, 0, row - top], source[order, 1, row - top]
                    term_re = coef_re * field_re - coef_im * field_im
                    term_im = coef_re * field_im + coef_im * field_re
                    real = term_re if real is None else real + term_re
                    imag = term_im if imag is None else imag + term_im
                outs += [real, imag]
            if later:
                for field in range(4):
                    levels[0, field, row - next_lowest] = outs[field]
            else:
                at = pl.ds(own_start(row), tiles, stride=SUBLANES)
                src_ref[0, at, :] = outs[0]
                src_ref[1, at, :] = outs[1]
                rec_ref[0, at, :] = outs[2]
                rec_ref[1, at, :] = -outs[3]
            if not 0 <= row < rows:
                continue
            value = outs[0] * outs[2] - outs[1] * outs[3]
            row_images.append(value)
            if not packed:
                image_refs[0][step, pl.ds(own_start(row), tiles, stride=SUBLANES), :] = value
            elif not later:
                first = images[0][row]
                even = jnp.where(in_low, first, pltpu.roll(value, width, 1))
                odd = jnp.where(in_low, pltpu.roll(first, width, 1), value)
                at = pl.ds(own(row), tiles, stride=rows)
                image_refs[0][at, :] = jnp.where(keeps_even, even, odd)
                image_refs[1][at, :] = jnp.where(keeps_even, odd, even)
        images.append(row_images)


def tiled(block):
    parts, rows, columns = block.shape
    split = block.reshape(parts, rows // SUBLANES, SUBLANES, columns // LANES, LANES)
    return split.transpose(0, 1, 3, 2, 4).reshape(parts, rows * columns // LANES, LANES)


def untiled(block, rows):
    parts, count, _ = block.shape
    tiles = count // rows
    split = block.reshape(parts, rows // SUBLANES, tiles, SUBLANES, LANES)
    return split.transpose(0, 1, 3, 2, 4).reshape(parts, rows, tiles * LANES)


def from_sides(block):
    count = lax.axis_size("lat")
    if count == 2:
        return [lax.ppermute(block, "lat", [(0, 1), (1, 0)])]
    return [
        lax.ppermute(block, "lat", [(i, i - side) for i in range(count) if 0 <= i - side < count]) for side in (-1, 1)
    ]


def partner(block, mask):
    return lax.ppermute(block, "freq", [(i, i ^ mask) for i in range(lax.axis_size("freq"))])


VMEM = pl.BlockSpec(memory_space=pltpu.VMEM)
COST = pl.CostEstimate(flops=1 << 26, bytes_accessed=1 << 22, transcendentals=0)


def call(kernel, shapes, *operands, mib=2, **options):
    single = not isinstance(shapes, list)
    outs = [jax.ShapeDtypeStruct(shape, jnp.float32) for shape in ([shapes] if single else shapes)]
    options.setdefault("in_specs", [VMEM] * len(operands))
    return pl.pallas_call(
        kernel,
        out_shape=outs[0] if single else outs,
        out_specs=VMEM if single else [VMEM] * len(outs),
        compiler_params=pltpu.CompilerParams(vmem_limit_bytes=mib << 20),
        **options,
    )(*operands)


def bundle_kernel(halo, two, *refs):
    layers, sides, out = refs[: -2 if two else -3], refs[-2 if two else -3 : -1], refs[-1]
    rows = layers[0].shape[0]
    out[:rows, :] = layers[0][...]
    if two:
        start = pl.multiple_of(lax.axis_index("lat") * (rows - halo), SUBLANES)
        out[rows : rows + halo, :] = sides[0][0, pl.ds(start, halo), :]
    else:
        out[rows : rows + halo, :] = sides[0][0, rows - halo :, :]
        out[rows + halo : rows + 2 * halo, :] = sides[1][0, :halo, :]
    after = rows + halo * len(sides)
    for step, layer in enumerate(layers[1:]):
        out[after + step * rows : after + (step + 1) * rows, :] = layer[...]


def beside_kernel(bit, mine, other, out):
    upper = ((lax.axis_index("freq") >> bit) & 1) != 0
    first, second = mine[...], other[...]
    out[...] = jnp.concatenate([jnp.where(upper, second, first), jnp.where(upper, first, second)], axis=1)


def stack_kernel(bit, mine, other, out):
    slot = (lax.axis_index("freq") >> bit) & 1
    for piece in range(mine.shape[0]):
        out[2 * piece + slot] = mine[piece]
        out[2 * piece + 1 - slot] = other[piece]


def gather_columns(block):
    count = lax.axis_size("freq")
    rows, width = block.shape
    bits = range(count.bit_length() - 1)
    inner = [b for b in bits if width << b < LANES]
    outer = [b for b in bits if width << b >= LANES][::-1]
    for b in inner:
        other = partner(block, 1 << b)
        shape = (rows, 2 * block.shape[1])
        block = call(functools.partial(beside_kernel, b), shape, block, other, cost_estimate=COST)
    block = block[None]
    parts = []
    for at, b in enumerate(outer):
        other = partner(block, (1 << b) | (1 if inner else 0))
        if at == len(outer) - 2:
            parts.append((block, ((b, False), (outer[-1], False))))
            parts.append((other, ((b, True), (outer[-1], False))))
        if b == outer[-1]:
            parts.append((other, ((b, True),)))
            return parts
        shape = (2 * block.shape[0], *block.shape[1:])
        block = call(functools.partial(stack_kernel, b), shape, block, other, cost_estimate=COST)


def halve_kernel(bit, held, came, keep, send):
    slot = (lax.axis_index("freq") >> bit) & 1
    for piece in range(keep.shape[0]):
        here, there = 2 * piece + slot, 2 * piece + 1 - slot
        send[piece] = held[there] + came[there]
        keep[piece] = held[here] + came[here]


def last_kernel(scale, held, came, out):
    total = (held[0] + came[0]) * scale
    width = out.shape[2]
    for step in range(out.shape[0]):
        out[step] = total[:, step * width : (step + 1) * width]


def scatter_sum(keep, send, rows, scale, out_shape):
    count = lax.axis_size("freq")
    pieces = count // 2
    held = keep.reshape(pieces, rows, LANES)
    came = partner(send, 1).reshape(pieces, rows, LANES)
    for b in range(1, count.bit_length() - 1):
        pieces //= 2
        shapes = [(pieces, rows, LANES)] * 2
        held, send = call(functools.partial(halve_kernel, b), shapes, held, came)
        came = partner(send, (1 << b) | 1)
    return call(functools.partial(last_kernel, scale), out_shape, held, came)


def shards(frequencies, slowness, src_field, rec_field):
    depth_steps, rows, width = slowness.shape
    tiles = src_field.shape[3] // LANES
    freq_count = lax.axis_size("freq")
    two = lax.axis_size("lat") == 2
    packed = depth_steps == 2 and width * depth_steps == LANES
    norm_factor = 1.0 / math.sqrt(frequencies.shape[0] * freq_count)
    halo = -(-REACH * (depth_steps - 1) // SUBLANES) * SUBLANES
    low, high = window(rows, depth_steps - 1, two)
    span = high + REACH - (low if two else low - REACH)
    later_span = window(rows, 1, two)[1] - window(rows, 1, two)[0]

    slow_sides = from_sides(slowness)
    src_sides = from_sides(src_field)
    rec_sides = from_sides(rec_field)
    coef_rows = (rows + halo * len(slow_sides)) + (depth_steps - 1) * rows
    layers = [slowness[z] for z in range(depth_steps)]
    kernel = functools.partial(bundle_kernel, halo, two)
    bundle = call(kernel, (coef_rows, width), *layers, *slow_sides)
    parts = gather_columns(bundle)

    def first_levels(own, sides, conjugate):
        fields = [tiled(x[0]) for x in (own, *sides)]
        kernel = functools.partial(first_kernel, rows, depth_steps, two, conjugate)
        return call(kernel, (TERMS, 2, span, tiles, LANES), *fields, mib=4, cost_estimate=COST)

    src_levels = first_levels(src_field, src_sides, False)
    rec_levels = first_levels(rec_field, rec_sides, True)

    coef_shape = (TERMS, 2, tiles, coef_rows, LANES)
    freq = frequencies.reshape(1, 1)
    coefs = []
    for part, shared in parts:
        coefs = [
            call(
                functools.partial(coefficient_kernel, shared),
                coef_shape,
                freq,
                part,
                *coefs,
                mib=8,
                input_output_aliases={2: 0} if coefs else {},
                cost_estimate=COST,
            )
        ]

    image_shape = (tiles * rows, LANES) if packed else (depth_steps, rows * tiles, LANES)
    field_shape = (2, rows * tiles, LANES)
    image_shapes = [image_shape] * (2 if packed else 1)
    setup = (rows, halo, depth_steps, two, packed, width)
    *image, src, rec = call(
        functools.partial(main_kernel, setup),
        [*image_shapes, field_shape, field_shape],
        coefs[0].reshape(TERMS, 2, tiles * coef_rows, LANES),
        src_levels,
        rec_levels,
        mib=16,
        scratch_shapes=[pltpu.VMEM((TERMS, 4, later_span, tiles, LANES), jnp.float32)],
    )

    if packed:
        depth_image = scatter_sum(*image, rows, norm_factor, (depth_steps, rows, width))
    else:
        whole = untiled(image[0], rows).reshape(depth_steps, rows, freq_count, width)
        pieces = whole.transpose(2, 0, 1, 3)
        depth_image = jnp.sum(lax.all_to_all(pieces, "freq", 0, 0, tiled=True), axis=0) * norm_factor
    return (depth_image, untiled(src, rows)[None], untiled(rec, rows)[None])


def solution(mesh):
    placed = (
        P("freq"),
        P(None, "lat", "freq"),
        P("freq", None, "lat", None),
        P("freq", None, "lat", None),
    )
    return jax.shard_map(
        shards,
        mesh=mesh,
        in_specs=placed,
        out_specs=(
            P(None, "lat", "freq"),
            P("freq", None, "lat", None),
            P("freq", None, "lat", None),
        ),
        check_vma=False,
    )
```

```python
import functools
import math

import jax
import jax.numpy as jnp
from jax import lax
from jax.experimental import pallas as pl
from jax.experimental.pallas import tpu as pltpu
from jax.sharding import PartitionSpec as P

TERMS = 8
REACH = TERMS - 1
LANES = 128
SUBLANES = 8

damping = 0.1

SINE = (0.5, -0.010416666045784950, 6.510379898820e-05, -1.9366727e-07, 3.26248263e-10)


def horner(powers, x):
    total = powers[-1] * x + powers[-2]
    for power in powers[-3::-1]:
        total = total * x + power
    return total


def node_phases(wavenum):
    square = wavenum * wavenum
    absorb = damping * square
    absorb_square = absorb * absorb
    phases = []
    for node in range(TERMS):
        angle = math.pi * (node + 0.5) / TERMS
        excess = square - angle * angle
        modulus_square = excess * excess + absorb_square
        doubled = modulus_square * lax.rsqrt(modulus_square) + jnp.abs(excess)
        inverse = lax.rsqrt(doubled)
        larger = doubled * inverse
        smaller = absorb * inverse
        propagating = excess >= 0
        real_part = jnp.where(propagating, larger, smaller)
        imag_part = jnp.where(propagating, smaller, larger)
        attenuation = jnp.exp(imag_part * -math.sqrt(0.5))
        sine = real_part * horner(SINE, real_part * real_part)
        sine_square = sine * sine
        rest = 2.0 - sine_square
        phase_re = attenuation * (1.0 - sine_square)
        phase_im = attenuation * (sine * (rest * lax.rsqrt(rest)))
        phases.append((phase_re, phase_im))
    return phases


def cosine_sums(values):
    half = TERMS // 2
    both = [values[j] + values[TERMS - 1 - j] for j in range(half)]
    apart = [values[j] - values[TERMS - 1 - j] for j in range(half)]
    outer, inner = both[0] + both[3], both[1] + both[2]
    outer_gap, inner_gap = both[0] - both[3], both[1] - both[2]
    scale = 2.0 / TERMS
    c1, c2, c3 = (scale * math.cos(math.pi * m / 8) for m in (1, 2, 3))
    sums = [None] * TERMS
    sums[0] = (1.0 / TERMS) * (outer + inner)
    sums[4] = c2 * (outer - inner)
    sums[2] = c1 * outer_gap + c3 * inner_gap
    sums[6] = c3 * outer_gap - c1 * inner_gap
    for order in range(1, TERMS, 2):
        row = [scale * math.cos(order * math.pi * (j + 0.5) / TERMS) for j in range(half)]
        sums[order] = (row[0] * apart[0] + row[1] * apart[1]) + (row[2] * apart[2] + row[3] * apart[3])
    return sums


def window(rows, later, two):
    return (0 if two else -REACH * later), rows + REACH * later


def strided(row, tiles):
    return (row // SUBLANES) * SUBLANES * tiles + row % SUBLANES


def either(flip, here, there):
    return here + flip * (there - here)


def spreader(tiles):
    lane = lax.broadcasted_iota(jnp.int32, (tiles, LANES), 1)
    tile = lax.broadcasted_iota(jnp.int32, (tiles, LANES), 0)
    first_lane, last_lane = lane == 0, lane == LANES - 1
    first_tile, last_tile = tile == 0, tile == tiles - 1

    def spread(values):
        left = pltpu.roll(values, 1, 1)
        right = pltpu.roll(values, LANES - 1, 1)
        before = jnp.where(first_tile, 0.0, pltpu.roll(left, 1, 0))
        after = jnp.where(last_tile, 0.0, pltpu.roll(right, tiles - 1, 0))
        left = jnp.where(first_lane, before, left)
        right = jnp.where(last_lane, after, right)
        return (values + values) + (left + right)

    return spread


def chebyshev(levels, fields, low, high, lowest, rows, two):
    spread = spreader(levels.shape[3])
    if not two:
        lat = lax.axis_index("lat")
        inside_low = (lat > 0).astype(jnp.float32)
        inside_high = (lat < lax.axis_size("lat") - 1).astype(jnp.float32)
    for order in range(1, TERMS):
        left = TERMS - 1 - order
        begin, end = (low if two else low - left), high + left
        above = [None if two else spread(levels[order - 1, f, begin - 1 - lowest]) for f in fields]
        here = [spread(levels[order - 1, f, begin - lowest]) for f in fields]
        for row in range(begin, end):
            for k, f in enumerate(fields):
                below = spread(levels[order - 1, f, row + 1 - lowest])
                total = (here[k] + here[k]) + below
                if above[k] is not None:
                    total = total + above[k]
                centre = levels[order - 1, f, row - lowest]
                if order == 1:
                    value = 0.125 * total - centre
                else:
                    value = (0.25 * total - (centre + centre)) - levels[order - 2, f, row - lowest]
                if not two and row < 0:
                    value = value * inside_low
                if not two and row >= rows:
                    value = value * inside_high
                levels[order, f, row - lowest] = value
                above[k], here[k] = here[k], below


def first_kernel(rows, depth_steps, two, conjugate, *refs):
    fields, levels = refs[:-1], refs[-1]
    tiles = levels.shape[3]
    flip = lax.axis_index("lat")
    low, high = window(rows, depth_steps - 1, two)
    lowest = low if two else low - REACH
    for row in range(lowest, high + REACH):
        if two:
            side = 0 if row < rows else 1
            ref, near = fields[side], row - side * rows
            start = either(flip, strided(near, tiles), strided(rows - 1 - near, tiles))
        else:
            side = 1 if row < 0 else 2 if row >= rows else 0
            ref, start = fields[side], strided(row + (0, rows, -rows)[side], tiles)
        for part in range(2):
            value = ref[part, pl.ds(start, tiles, stride=SUBLANES), :]
            levels[0, part, row - lowest] = -value if part and conjugate else value
    chebyshev(levels, (0, 1), low, high, lowest, rows, two)


def coefficient_kernel(shared, tiles, *refs):
    freq_ref, slow_ref, out_ref = refs[0], refs[1], refs[-1]
    count, rows, _ = slow_ref.shape
    slot = 0
    for bit, other in shared:
        own = (lax.axis_index("freq") >> bit) & 1
        slot = 2 * slot + (1 - own if other else own)
    freq = freq_ref[...]

    def body(piece, carry):
        place = (piece << len(shared)) + slot
        for start in range(0, rows, SUBLANES):
            phases = node_phases(freq * slow_ref[piece, start : start + SUBLANES, :])
            for part in range(2):
                for order, value in enumerate(cosine_sums([p[part] for p in phases])):
                    out_ref[order, part, pl.ds(start * tiles + place, SUBLANES, stride=tiles), :] = value
        return carry

    lax.fori_loop(0, count, body, 0)


def main_kernel(setup, coef_ref, src_levels, rec_levels, *refs):
    rows, halo, depth_steps, two, packed, width = setup
    image_refs, (src_ref, rec_ref, levels) = refs[:-3], refs[-3:]
    tiles = levels.shape[3]
    flip = lax.axis_index("lat")
    lane = lax.broadcasted_iota(jnp.int32, (tiles, LANES), 1)
    tile = lax.broadcasted_iota(jnp.int32, (tiles, LANES), 0)
    in_low = lane < width
    if packed:
        parity, me, count = tile * 0, lax.axis_index("freq"), lax.axis_size("freq")
        for bit in range(count.bit_length() - 1):
            parity = parity ^ (tile >> bit) ^ (me >> bit)
        keeps_even = (parity & 1) == 0

    def own(row):
        return either(flip, row, rows - 1 - row) if two else row

    def own_start(row):
        return either(flip, strided(row, tiles), strided(rows - 1 - row, tiles)) if two else strided(row, tiles)

    def coef_row(step, row):
        sides = 1 if two else 2
        if step:
            return rows + sides * halo + (step - 1) * rows + own(row)
        if 0 <= row < rows:
            return own(row)
        if two:
            return rows + either(flip, row - rows, halo - 1 - (row - rows))
        return rows + halo + (row if row < 0 else row - rows)

    images = []
    for step in range(depth_steps):
        later = depth_steps - 1 - step
        low, high = window(rows, later, two)
        lowest = window(rows, max(later, 1), two)[0]
        if step:

            def pair_fields(pair, carry, low=low, high=high, lowest=lowest):
                chebyshev(levels, (2 * pair, 2 * pair + 1), low, high, lowest, rows, two)
                return carry

            lax.fori_loop(0, 2, pair_fields, 0)
        top = low if two else low - REACH
        next_lowest = window(rows, max(later - 1, 1), two)[0]
        row_images = []
        for row in range(low, high):
            start = pl.multiple_of(coef_row(step, row) * tiles, SUBLANES)
            coefs = [
                [coef_ref[order, part, pl.ds(start, tiles), :] for part in range(2)]
                for order in range(TERMS)
            ]
            outs = []
            for pair in range(2):
                real = imag = None
                for order, (coef_re, coef_im) in enumerate(coefs):
                    if step:
                        field_re = levels[order, 2 * pair, row - lowest]
                        field_im = levels[order, 2 * pair + 1, row - lowest]
                    else:
                        source = rec_levels if pair else src_levels
                        field_re, field_im = source[order, 0, row - top], source[order, 1, row - top]
                    term_re = coef_re * field_re - coef_im * field_im
                    term_im = coef_re * field_im + coef_im * field_re
                    real = term_re if real is None else real + term_re
                    imag = term_im if imag is None else imag + term_im
                outs += [real, imag]
            if later:
                for field in range(4):
                    levels[0, field, row - next_lowest] = outs[field]
            else:
                at = pl.ds(own_start(row), tiles, stride=SUBLANES)
                src_ref[0, at, :] = outs[0]
                src_ref[1, at, :] = outs[1]
                rec_ref[0, at, :] = outs[2]
                rec_ref[1, at, :] = -outs[3]
            if not 0 <= row < rows:
                continue
            value = outs[0] * outs[2] - outs[1] * outs[3]
            row_images.append(value)
            if not packed:
                image_refs[0][step, pl.ds(own_start(row), tiles, stride=SUBLANES), :] = value
            elif not later:
                first = images[0][row]
                even = jnp.where(in_low, first, pltpu.roll(value, width, 1))
                odd = jnp.where(in_low, pltpu.roll(first, width, 1), value)
                at = pl.ds(own(row), tiles, stride=rows)
                image_refs[0][at, :] = jnp.where(keeps_even, even, odd)
                image_refs[1][at, :] = jnp.where(keeps_even, odd, even)
        images.append(row_images)


def tiled(block):
    parts, rows, columns = block.shape
    split = block.reshape(parts, rows // SUBLANES, SUBLANES, columns // LANES, LANES)
    return split.transpose(0, 1, 3, 2, 4).reshape(parts, rows * columns // LANES, LANES)


def untiled(block, rows):
    parts, count, _ = block.shape
    tiles = count // rows
    split = block.reshape(parts, rows // SUBLANES, tiles, SUBLANES, LANES)
    return split.transpose(0, 1, 3, 2, 4).reshape(parts, rows, tiles * LANES)


def from_sides(block):
    count = lax.axis_size("lat")
    if count == 2:
        return [lax.ppermute(block, "lat", [(0, 1), (1, 0)])]
    return [
        lax.ppermute(block, "lat", [(i, i - side) for i in range(count) if 0 <= i - side < count]) for side in (-1, 1)
    ]


def partner(block, mask):
    return lax.ppermute(block, "freq", [(i, i ^ mask) for i in range(lax.axis_size("freq"))])


VMEM = pl.BlockSpec(memory_space=pltpu.VMEM)
COST = pl.CostEstimate(flops=1 << 26, bytes_accessed=1 << 22, transcendentals=0)


def call(kernel, shapes, *operands, mib=2, **options):
    single = not isinstance(shapes, list)
    outs = [jax.ShapeDtypeStruct(shape, jnp.float32) for shape in ([shapes] if single else shapes)]
    options.setdefault("in_specs", [VMEM] * len(operands))
    return pl.pallas_call(
        kernel,
        out_shape=outs[0] if single else outs,
        out_specs=VMEM if single else [VMEM] * len(outs),
        compiler_params=pltpu.CompilerParams(vmem_limit_bytes=mib << 20),
        **options,
    )(*operands)


def bundle_kernel(halo, two, *refs):
    layers, sides, out = refs[: -2 if two else -3], refs[-2 if two else -3 : -1], refs[-1]
    rows = layers[0].shape[0]
    out[:rows, :] = layers[0][...]
    if two:
        start = pl.multiple_of(lax.axis_index("lat") * (rows - halo), SUBLANES)
        out[rows : rows + halo, :] = sides[0][0, pl.ds(start, halo), :]
    else:
        out[rows : rows + halo, :] = sides[0][0, rows - halo :, :]
        out[rows + halo : rows + 2 * halo, :] = sides[1][0, :halo, :]
    after = rows + halo * len(sides)
    for step, layer in enumerate(layers[1:]):
        out[after + step * rows : after + (step + 1) * rows, :] = layer[...]


def pair_kernel(halo, *refs):
    layers, (core, out, edge) = refs[:-3], refs[-3:]
    rows = layers[0].shape[0]
    upper = (lax.axis_index("freq") & 1) != 0
    for step, layer in enumerate(layers):
        mine, other = layer[...], core[step]
        pair = jnp.concatenate([jnp.where(upper, other, mine), jnp.where(upper, mine, other)], axis=1)
        out[step * rows : (step + 1) * rows, :] = pair
    start = pl.multiple_of((1 - lax.axis_index("lat")) * (rows - halo), SUBLANES)
    edge[...] = out[pl.ds(start, halo), :]


def tile_kernel(pair, edge, freq, out, freq_out):
    halo, rows = edge.shape[0], out.shape[0] - edge.shape[0]
    first = rows // 2
    out[:first, :] = pair[:first, :]
    out[first : first + halo, :] = edge[...]
    out[first + halo :, :] = pair[first:, :]
    freq_out[...] = freq[...]


def beside_kernel(bit, mine, other, out):
    upper = ((lax.axis_index("freq") >> bit) & 1) != 0
    first, second = mine[...], other[...]
    out[...] = jnp.concatenate([jnp.where(upper, second, first), jnp.where(upper, first, second)], axis=1)


def stack_kernel(bit, mine, other, out):
    slot = (lax.axis_index("freq") >> bit) & 1
    for piece in range(mine.shape[0]):
        out[2 * piece + slot] = mine[piece]
        out[2 * piece + 1 - slot] = other[piece]


def gather_columns(block, done=0):
    count = lax.axis_size("freq")
    rows, width = block.shape
    width >>= done
    bits = range(count.bit_length() - 1)
    inner = [b for b in bits if width << b < LANES]
    outer = [b for b in bits if width << b >= LANES][::-1]
    for b in inner[done:]:
        other = partner(block, 1 << b)
        shape = (rows, 2 * block.shape[1])
        block = call(functools.partial(beside_kernel, b), shape, block, other, cost_estimate=COST)
    block = block[None]
    parts = []
    for at, b in enumerate(outer):
        other = partner(block, (1 << b) | (1 if inner else 0))
        if at == len(outer) - 2:
            parts.append((block, ((b, False), (outer[-1], False))))
            parts.append((other, ((b, True), (outer[-1], False))))
        if b == outer[-1]:
            parts.append((other, ((b, True),)))
            return parts
        shape = (2 * block.shape[0], *block.shape[1:])
        block = call(functools.partial(stack_kernel, b), shape, block, other, cost_estimate=COST)


def halve_kernel(bit, held, came, keep, send):
    slot = (lax.axis_index("freq") >> bit) & 1
    for piece in range(keep.shape[0]):
        here, there = 2 * piece + slot, 2 * piece + 1 - slot
        send[piece] = held[there] + came[there]
        keep[piece] = held[here] + came[here]


def last_kernel(scale, held, came, out):
    total = (held[0] + came[0]) * scale
    width = out.shape[2]
    for step in range(out.shape[0]):
        out[step] = total[:, step * width : (step + 1) * width]


def scatter_sum(keep, send, rows, scale, out_shape):
    count = lax.axis_size("freq")
    pieces = count // 2
    held = keep.reshape(pieces, rows, LANES)
    came = partner(send, 1).reshape(pieces, rows, LANES)
    for b in range(1, count.bit_length() - 1):
        pieces //= 2
        shapes = [(pieces, rows, LANES)] * 2
        held, send = call(functools.partial(halve_kernel, b), shapes, held, came)
        came = partner(send, (1 << b) | 1)
    return call(functools.partial(last_kernel, scale), out_shape, held, came)


def shards(frequencies, slowness, src_field, rec_field):
    depth_steps, rows, width = slowness.shape
    tiles = src_field.shape[3] // LANES
    freq_count = lax.axis_size("freq")
    two = lax.axis_size("lat") == 2
    packed = depth_steps == 2 and width * depth_steps == LANES
    norm_factor = 1.0 / math.sqrt(frequencies.shape[0] * freq_count)
    halo = -(-REACH * (depth_steps - 1) // SUBLANES) * SUBLANES
    low, high = window(rows, depth_steps - 1, two)
    span = high + REACH - (low if two else low - REACH)
    later_span = window(rows, 1, two)[1] - window(rows, 1, two)[0]

    src_sides = from_sides(src_field)
    rec_sides = from_sides(rec_field)
    coef_rows = depth_steps * rows + halo * len(src_sides)
    layers = [slowness[z] for z in range(depth_steps)]
    freq = jnp.broadcast_to(frequencies, (SUBLANES, LANES))
    if two and 2 * width == LANES and depth_steps == 2:
        core = partner(slowness, 1)
        shapes = [(depth_steps * rows, LANES), (halo, LANES)]
        pair, edge = call(functools.partial(pair_kernel, halo), shapes, *layers, core, cost_estimate=COST)
        (edge,) = from_sides(edge)
        shapes = [(coef_rows, LANES), (SUBLANES, LANES)]
        block, freq = call(tile_kernel, shapes, pair, edge, freq, cost_estimate=COST)
        parts = gather_columns(block, done=1)
    else:
        slow_sides = from_sides(slowness)
        kernel = functools.partial(bundle_kernel, halo, two)
        bundle = call(kernel, (coef_rows, width), *layers, *slow_sides)
        parts = gather_columns(bundle)

    def first_levels(own, sides, conjugate):
        fields = [tiled(x[0]) for x in (own, *sides)]
        kernel = functools.partial(first_kernel, rows, depth_steps, two, conjugate)
        return call(kernel, (TERMS, 2, span, tiles, LANES), *fields, mib=4, cost_estimate=COST)

    src_levels = first_levels(src_field, src_sides, False)
    rec_levels = first_levels(rec_field, rec_sides, True)

    coef_shape = (TERMS, 2, coef_rows * tiles, LANES)
    coefs = []
    for part, shared in parts:
        coefs = [
            call(
                functools.partial(coefficient_kernel, shared, tiles),
                coef_shape,
                freq,
                part,
                *coefs,
                mib=8,
                input_output_aliases={2: 0} if coefs else {},
                cost_estimate=COST,
            )
        ]

    image_shape = (tiles * rows, LANES) if packed else (depth_steps, rows * tiles, LANES)
    field_shape = (2, rows * tiles, LANES)
    image_shapes = [image_shape] * (2 if packed else 1)
    setup = (rows, halo, depth_steps, two, packed, width)
    *image, src, rec = call(
        functools.partial(main_kernel, setup),
        [*image_shapes, field_shape, field_shape],
        coefs[0],
        src_levels,
        rec_levels,
        mib=16,
        scratch_shapes=[pltpu.VMEM((TERMS, 4, later_span, tiles, LANES), jnp.float32)],
    )

    if packed:
        depth_image = scatter_sum(*image, rows, norm_factor, (depth_steps, rows, width))
    else:
        whole = untiled(image[0], rows).reshape(depth_steps, rows, freq_count, width)
        pieces = whole.transpose(2, 0, 1, 3)
        depth_image = jnp.sum(lax.all_to_all(pieces, "freq", 0, 0, tiled=True), axis=0) * norm_factor
    return (depth_image, untiled(src, rows)[None], untiled(rec, rows)[None])


def solution(mesh):
    placed = (
        P("freq"),
        P(None, "lat", "freq"),
        P("freq", None, "lat", None),
        P("freq", None, "lat", None),
    )
    return jax.shard_map(
        shards,
        mesh=mesh,
        in_specs=placed,
        out_specs=(
            P(None, "lat", "freq"),
            P("freq", None, "lat", None),
            P("freq", None, "lat", None),
        ),
        check_vma=False,
    )
```

```python
import functools
import math

import jax
import jax.numpy as jnp
from jax import lax
from jax.experimental import pallas as pl
from jax.experimental.pallas import tpu as pltpu
from jax.sharding import PartitionSpec as P

TERMS = 8
REACH = TERMS - 1
LANES = 128
SUBLANES = 8

damping = 0.1

SINE = (0.5, -0.010416666045784950, 6.510379898820e-05, -1.9366727e-07, 3.26248263e-10)


def horner(powers, x):
    total = powers[-1] * x + powers[-2]
    for power in powers[-3::-1]:
        total = total * x + power
    return total


def node_phases(wavenum):
    square = wavenum * wavenum
    absorb = damping * square
    absorb_square = absorb * absorb
    phases = []
    for node in range(TERMS):
        angle = math.pi * (node + 0.5) / TERMS
        excess = square - angle * angle
        modulus_square = excess * excess + absorb_square
        doubled = modulus_square * lax.rsqrt(modulus_square) + jnp.abs(excess)
        inverse = lax.rsqrt(doubled)
        larger = doubled * inverse
        smaller = absorb * inverse
        propagating = excess >= 0
        real_part = jnp.where(propagating, larger, smaller)
        imag_part = jnp.where(propagating, smaller, larger)
        attenuation = jnp.exp2(imag_part * (-math.sqrt(0.5) / math.log(2.0)))
        sine = real_part * horner(SINE, real_part * real_part)
        sine_square = sine * sine
        rest = 2.0 - sine_square
        phase_re = attenuation * (1.0 - sine_square)
        phase_im = attenuation * (sine * (rest * lax.rsqrt(rest)))
        phases.append((phase_re, phase_im))
    return phases


def cosine_sums(values):
    half = TERMS // 2
    both = [values[j] + values[TERMS - 1 - j] for j in range(half)]
    apart = [values[j] - values[TERMS - 1 - j] for j in range(half)]
    outer, inner = both[0] + both[3], both[1] + both[2]
    outer_gap, inner_gap = both[0] - both[3], both[1] - both[2]
    scale = 2.0 / TERMS
    c1, c2, c3 = (scale * math.cos(math.pi * m / 8) for m in (1, 2, 3))
    sums = [None] * TERMS
    sums[0] = (1.0 / TERMS) * (outer + inner)
    sums[4] = c2 * (outer - inner)
    sums[2] = c1 * outer_gap + c3 * inner_gap
    sums[6] = c3 * outer_gap - c1 * inner_gap
    for order in range(1, TERMS, 2):
        row = [scale * math.cos(order * math.pi * (j + 0.5) / TERMS) for j in range(half)]
        sums[order] = (row[0] * apart[0] + row[1] * apart[1]) + (row[2] * apart[2] + row[3] * apart[3])
    return sums


def window(rows, later, two):
    return (0 if two else -REACH * later), rows + REACH * later


def strided(row, tiles):
    return (row // SUBLANES) * SUBLANES * tiles + row % SUBLANES


def either(flip, here, there):
    return here + flip * (there - here)


def spreader(tiles):
    lane = lax.broadcasted_iota(jnp.int32, (tiles, LANES), 1)
    tile = lax.broadcasted_iota(jnp.int32, (tiles, LANES), 0)
    first_lane, last_lane = lane == 0, lane == LANES - 1
    first_tile, last_tile = tile == 0, tile == tiles - 1

    def spread(values):
        left = pltpu.roll(values, 1, 1)
        right = pltpu.roll(values, LANES - 1, 1)
        before = jnp.where(first_tile, 0.0, pltpu.roll(left, 1, 0))
        after = jnp.where(last_tile, 0.0, pltpu.roll(right, tiles - 1, 0))
        left = jnp.where(first_lane, before, left)
        right = jnp.where(last_lane, after, right)
        return (values + values) + (left + right)

    return spread


def chebyshev(levels, fields, low, high, lowest, rows, two):
    spread = spreader(levels.shape[3])
    if not two:
        lat = lax.axis_index("lat")
        inside_low = (lat > 0).astype(jnp.float32)
        inside_high = (lat < lax.axis_size("lat") - 1).astype(jnp.float32)
    for order in range(1, TERMS):
        left = TERMS - 1 - order
        begin, end = (low if two else low - left), high + left
        above = [None if two else spread(levels[order - 1, f, begin - 1 - lowest]) for f in fields]
        here = [spread(levels[order - 1, f, begin - lowest]) for f in fields]
        for row in range(begin, end):
            for k, f in enumerate(fields):
                below = spread(levels[order - 1, f, row + 1 - lowest])
                total = (here[k] + here[k]) + below
                if above[k] is not None:
                    total = total + above[k]
                centre = levels[order - 1, f, row - lowest]
                if order == 1:
                    value = 0.125 * total - centre
                else:
                    value = (0.25 * total - (centre + centre)) - levels[order - 2, f, row - lowest]
                if not two and row < 0:
                    value = value * inside_low
                if not two and row >= rows:
                    value = value * inside_high
                levels[order, f, row - lowest] = value
                above[k], here[k] = here[k], below


def first_kernel(rows, depth_steps, two, conjugate, *refs):
    fields, levels = refs[:-1], refs[-1]
    tiles = levels.shape[3]
    flip = lax.axis_index("lat")
    low, high = window(rows, depth_steps - 1, two)
    lowest = low if two else low - REACH
    for row in range(lowest, high + REACH):
        if two:
            side = 0 if row < rows else 1
            ref, near = fields[side], row - side * rows
            start = either(flip, strided(near, tiles), strided(rows - 1 - near, tiles))
        else:
            side = 1 if row < 0 else 2 if row >= rows else 0
            ref, start = fields[side], strided(row + (0, rows, -rows)[side], tiles)
        for part in range(2):
            value = ref[part, pl.ds(start, tiles, stride=SUBLANES), :]
            levels[0, part, row - lowest] = -value if part and conjugate else value
    chebyshev(levels, (0, 1), low, high, lowest, rows, two)


def coefficient_kernel(shared, tiles, *refs):
    freq_ref, slow_ref, out_ref = refs[0], refs[1], refs[-1]
    count, rows, _ = slow_ref.shape
    slot = 0
    for bit, other in shared:
        own = (lax.axis_index("freq") >> bit) & 1
        slot = 2 * slot + (1 - own if other else own)
    freq = freq_ref[...]

    def body(piece, carry):
        place = (piece << len(shared)) + slot
        for start in range(0, rows, SUBLANES):
            phases = node_phases(freq * slow_ref[piece, start : start + SUBLANES, :])
            for part in range(2):
                for order, value in enumerate(cosine_sums([p[part] for p in phases])):
                    out_ref[order, part, pl.ds(start * tiles + place, SUBLANES, stride=tiles), :] = value
        return carry

    lax.fori_loop(0, count, body, 0)


def main_kernel(setup, coef_ref, src_levels, rec_levels, *refs):
    rows, halo, depth_steps, two, packed, width = setup
    image_refs, (final_ref, levels) = refs[:-2], refs[-2:]
    tiles = levels.shape[3]
    flip = lax.axis_index("lat")
    lane = lax.broadcasted_iota(jnp.int32, (tiles, LANES), 1)
    tile = lax.broadcasted_iota(jnp.int32, (tiles, LANES), 0)
    in_low = lane < width
    if packed:
        parity, me, count = tile * 0, lax.axis_index("freq"), lax.axis_size("freq")
        for bit in range(count.bit_length() - 1):
            parity = parity ^ (tile >> bit) ^ (me >> bit)
        keeps_even = (parity & 1) == 0

    def own(row):
        return either(flip, row, rows - 1 - row) if two else row

    def own_start(row):
        return either(flip, strided(row, tiles), strided(rows - 1 - row, tiles)) if two else strided(row, tiles)

    def coef_row(step, row):
        sides = 1 if two else 2
        if step:
            return rows + sides * halo + (step - 1) * rows + own(row)
        if 0 <= row < rows:
            return own(row)
        if two:
            return rows + either(flip, row - rows, halo - 1 - (row - rows))
        return rows + halo + (row if row < 0 else row - rows)

    images = []
    for step in range(depth_steps):
        later = depth_steps - 1 - step
        low, high = window(rows, later, two)
        lowest = window(rows, max(later, 1), two)[0]
        if step:

            def pair_fields(pair, carry, low=low, high=high, lowest=lowest):
                chebyshev(levels, (2 * pair, 2 * pair + 1), low, high, lowest, rows, two)
                return carry

            lax.fori_loop(0, 2, pair_fields, 0)
        top = low if two else low - REACH
        next_lowest = window(rows, max(later - 1, 1), two)[0]
        row_images = []
        for row in range(low, high):
            start = pl.multiple_of(coef_row(step, row) * tiles, SUBLANES)
            coefs = [
                [coef_ref[order, part, pl.ds(start, tiles), :] for part in range(2)]
                for order in range(TERMS)
            ]
            outs = []
            for pair in range(2):
                real = imag = None
                for order, (coef_re, coef_im) in enumerate(coefs):
                    if step:
                        field_re = levels[order, 2 * pair, row - lowest]
                        field_im = levels[order, 2 * pair + 1, row - lowest]
                    else:
                        source = rec_levels if pair else src_levels
                        field_re, field_im = source[order, 0, row - top], source[order, 1, row - top]
                    term_re = coef_re * field_re - coef_im * field_im
                    term_im = coef_re * field_im + coef_im * field_re
                    real = term_re if real is None else real + term_re
                    imag = term_im if imag is None else imag + term_im
                outs += [real, imag]
            if later:
                for field in range(4):
                    levels[0, field, row - next_lowest] = outs[field]
            else:
                for field in range(4):
                    final_ref[field, row] = outs[field]
            if not 0 <= row < rows:
                continue
            value = outs[0] * outs[2] - outs[1] * outs[3]
            row_images.append(value)
            if not packed:
                image_refs[0][step, pl.ds(own_start(row), tiles, stride=SUBLANES), :] = value
            elif not later:
                first = images[0][row]
                even = jnp.where(in_low, first, pltpu.roll(value, width, 1))
                odd = jnp.where(in_low, pltpu.roll(first, width, 1), value)
                at = pl.ds(own(row), tiles, stride=rows)
                image_refs[0][at, :] = jnp.where(keeps_even, even, odd)
                image_refs[1][at, :] = jnp.where(keeps_even, odd, even)
        images.append(row_images)


def finish_kernel(two, final_ref, src_ref, rec_ref):
    _, rows, tiles, _ = final_ref.shape
    flip = lax.axis_index("lat")
    for row in range(rows):
        start = strided(row, tiles)
        if two:
            start = either(flip, start, strided(rows - 1 - row, tiles))
        at = pl.ds(start, tiles, stride=SUBLANES)
        src_ref[0, at, :] = final_ref[0, row]
        src_ref[1, at, :] = final_ref[1, row]
        rec_ref[0, at, :] = final_ref[2, row]
        rec_ref[1, at, :] = -final_ref[3, row]


def tiled(block):
    parts, rows, columns = block.shape
    split = block.reshape(parts, rows // SUBLANES, SUBLANES, columns // LANES, LANES)
    return split.transpose(0, 1, 3, 2, 4).reshape(parts, rows * columns // LANES, LANES)


def untiled(block, rows):
    parts, count, _ = block.shape
    tiles = count // rows
    split = block.reshape(parts, rows // SUBLANES, tiles, SUBLANES, LANES)
    return split.transpose(0, 1, 3, 2, 4).reshape(parts, rows, tiles * LANES)


def from_sides(block):
    count = lax.axis_size("lat")
    if count == 2:
        return [lax.ppermute(block, "lat", [(0, 1), (1, 0)])]
    return [
        lax.ppermute(block, "lat", [(i, i - side) for i in range(count) if 0 <= i - side < count]) for side in (-1, 1)
    ]


def partner(block, mask):
    return lax.ppermute(block, "freq", [(i, i ^ mask) for i in range(lax.axis_size("freq"))])


VMEM = pl.BlockSpec(memory_space=pltpu.VMEM)
COST = pl.CostEstimate(flops=1 << 26, bytes_accessed=1 << 22, transcendentals=0)


def call(kernel, shapes, *operands, mib=2, **options):
    single = not isinstance(shapes, list)
    outs = [jax.ShapeDtypeStruct(shape, jnp.float32) for shape in ([shapes] if single else shapes)]
    options.setdefault("in_specs", [VMEM] * len(operands))
    return pl.pallas_call(
        kernel,
        out_shape=outs[0] if single else outs,
        out_specs=VMEM if single else [VMEM] * len(outs),
        compiler_params=pltpu.CompilerParams(vmem_limit_bytes=mib << 20),
        **options,
    )(*operands)


def bundle_kernel(halo, two, *refs):
    layers, sides, out = refs[: -2 if two else -3], refs[-2 if two else -3 : -1], refs[-1]
    rows = layers[0].shape[0]
    out[:rows, :] = layers[0][...]
    if two:
        start = pl.multiple_of(lax.axis_index("lat") * (rows - halo), SUBLANES)
        out[rows : rows + halo, :] = sides[0][0, pl.ds(start, halo), :]
    else:
        out[rows : rows + halo, :] = sides[0][0, rows - halo :, :]
        out[rows + halo : rows + 2 * halo, :] = sides[1][0, :halo, :]
    after = rows + halo * len(sides)
    for step, layer in enumerate(layers[1:]):
        out[after + step * rows : after + (step + 1) * rows, :] = layer[...]


def pair_kernel(halo, *refs):
    layers, (core, out, edge) = refs[:-3], refs[-3:]
    rows = layers[0].shape[0]
    upper = (lax.axis_index("freq") & 1) != 0
    for step, layer in enumerate(layers):
        mine, other = layer[...], core[step]
        pair = jnp.concatenate([jnp.where(upper, other, mine), jnp.where(upper, mine, other)], axis=1)
        out[step * rows : (step + 1) * rows, :] = pair
    start = pl.multiple_of((1 - lax.axis_index("lat")) * (rows - halo), SUBLANES)
    edge[...] = out[pl.ds(start, halo), :]


def tile_kernel(pair, edge, freq, out, freq_out):
    halo, rows = edge.shape[0], out.shape[0] - edge.shape[0]
    first = rows // 2
    out[:first, :] = pair[:first, :]
    out[first : first + halo, :] = edge[...]
    out[first + halo :, :] = pair[first:, :]
    freq_out[...] = freq[...]


def beside_kernel(bit, mine, other, out):
    upper = ((lax.axis_index("freq") >> bit) & 1) != 0
    first, second = mine[...], other[...]
    out[...] = jnp.concatenate([jnp.where(upper, second, first), jnp.where(upper, first, second)], axis=1)


def stack_kernel(bit, mine, other, out):
    slot = (lax.axis_index("freq") >> bit) & 1
    for piece in range(mine.shape[0]):
        out[2 * piece + slot] = mine[piece]
        out[2 * piece + 1 - slot] = other[piece]


def gather_columns(block, done=0):
    count = lax.axis_size("freq")
    rows, width = block.shape
    width >>= done
    bits = range(count.bit_length() - 1)
    inner = [b for b in bits if width << b < LANES]
    outer = [b for b in bits if width << b >= LANES][::-1]
    for b in inner[done:]:
        other = partner(block, 1 << b)
        shape = (rows, 2 * block.shape[1])
        block = call(functools.partial(beside_kernel, b), shape, block, other, cost_estimate=COST)
    block = block[None]
    cross = 1 if inner else 0
    for b in outer[:-2]:
        other = partner(block, (1 << b) | cross)
        shape = (2 * block.shape[0], *block.shape[1:])
        block = call(functools.partial(stack_kernel, b), shape, block, other, cost_estimate=COST)
    high, low = outer[-2:]
    other = partner(block, (1 << high) | cross)
    near = partner(block, (1 << low) | cross)
    far = partner(other, (1 << low) | cross)
    return [
        (block, ((high, False), (low, False))),
        (other, ((high, True), (low, False))),
        (near, ((high, False), (low, True))),
        (far, ((high, True), (low, True))),
    ]


def halve_kernel(bit, held, came, keep, send):
    slot = (lax.axis_index("freq") >> bit) & 1
    for piece in range(keep.shape[0]):
        here, there = 2 * piece + slot, 2 * piece + 1 - slot
        send[piece] = held[there] + came[there]
        keep[piece] = held[here] + came[here]


def last_kernel(scale, held, came, out):
    total = (held[0] + came[0]) * scale
    width = out.shape[2]
    for step in range(out.shape[0]):
        out[step] = total[:, step * width : (step + 1) * width]


def scatter_sum(keep, send, rows, scale, out_shape):
    count = lax.axis_size("freq")
    pieces = count // 2
    held = keep.reshape(pieces, rows, LANES)
    came = partner(send, 1).reshape(pieces, rows, LANES)
    for b in range(1, count.bit_length() - 1):
        pieces //= 2
        shapes = [(pieces, rows, LANES)] * 2
        held, send = call(functools.partial(halve_kernel, b), shapes, held, came)
        came = partner(send, (1 << b) | 1)
    return call(functools.partial(last_kernel, scale), out_shape, held, came)


def shards(frequencies, slowness, src_field, rec_field):
    depth_steps, rows, width = slowness.shape
    tiles = src_field.shape[3] // LANES
    freq_count = lax.axis_size("freq")
    two = lax.axis_size("lat") == 2
    packed = depth_steps == 2 and width * depth_steps == LANES
    norm_factor = 1.0 / math.sqrt(frequencies.shape[0] * freq_count)
    halo = -(-REACH * (depth_steps - 1) // SUBLANES) * SUBLANES
    low, high = window(rows, depth_steps - 1, two)
    span = high + REACH - (low if two else low - REACH)
    later_span = window(rows, 1, two)[1] - window(rows, 1, two)[0]

    src_sides = from_sides(src_field)
    rec_sides = from_sides(rec_field)
    coef_rows = depth_steps * rows + halo * len(src_sides)
    layers = [slowness[z] for z in range(depth_steps)]
    freq = jnp.broadcast_to(frequencies, (SUBLANES, LANES))
    if two and 2 * width == LANES and depth_steps == 2:
        core = partner(slowness, 1)
        shapes = [(depth_steps * rows, LANES), (halo, LANES)]
        pair, edge = call(functools.partial(pair_kernel, halo), shapes, *layers, core, cost_estimate=COST)
        (edge,) = from_sides(edge)
        shapes = [(coef_rows, LANES), (SUBLANES, LANES)]
        block, freq = call(tile_kernel, shapes, pair, edge, freq, cost_estimate=COST)
        parts = gather_columns(block, done=1)
    else:
        slow_sides = from_sides(slowness)
        kernel = functools.partial(bundle_kernel, halo, two)
        bundle = call(kernel, (coef_rows, width), *layers, *slow_sides)
        parts = gather_columns(bundle)

    def first_levels(own, sides, conjugate):
        fields = [tiled(x[0]) for x in (own, *sides)]
        kernel = functools.partial(first_kernel, rows, depth_steps, two, conjugate)
        return call(kernel, (TERMS, 2, span, tiles, LANES), *fields, mib=4, cost_estimate=COST)

    src_levels = first_levels(src_field, src_sides, False)
    rec_levels = first_levels(rec_field, rec_sides, True)

    coef_shape = (TERMS, 2, coef_rows * tiles, LANES)
    coefs = []
    for part, shared in parts:
        coefs = [
            call(
                functools.partial(coefficient_kernel, shared, tiles),
                coef_shape,
                freq,
                part,
                *coefs,
                mib=8,
                input_output_aliases={2: 0} if coefs else {},
                cost_estimate=COST,
            )
        ]

    image_shape = (tiles * rows, LANES) if packed else (depth_steps, rows * tiles, LANES)
    field_shape = (2, rows * tiles, LANES)
    image_shapes = [image_shape] * (2 if packed else 1)
    setup = (rows, halo, depth_steps, two, packed, width)
    *image, final = call(
        functools.partial(main_kernel, setup),
        [*image_shapes, (4, rows, tiles, LANES)],
        coefs[0],
        src_levels,
        rec_levels,
        mib=16,
        scratch_shapes=[pltpu.VMEM((TERMS, 4, later_span, tiles, LANES), jnp.float32)],
    )

    src, rec = call(functools.partial(finish_kernel, two), [field_shape] * 2, final, mib=4, cost_estimate=COST)

    if packed:
        depth_image = scatter_sum(*image, rows, norm_factor, (depth_steps, rows, width))
    else:
        whole = untiled(image[0], rows).reshape(depth_steps, rows, freq_count, width)
        pieces = whole.transpose(2, 0, 1, 3)
        depth_image = jnp.sum(lax.all_to_all(pieces, "freq", 0, 0, tiled=True), axis=0) * norm_factor
    return (depth_image, untiled(src, rows)[None], untiled(rec, rows)[None])


def solution(mesh):
    placed = (
        P("freq"),
        P(None, "lat", "freq"),
        P("freq", None, "lat", None),
        P("freq", None, "lat", None),
    )
    return jax.shard_map(
        shards,
        mesh=mesh,
        in_specs=placed,
        out_specs=(
            P(None, "lat", "freq"),
            P("freq", None, "lat", None),
            P("freq", None, "lat", None),
        ),
        check_vma=False,
    )
```

```python
import functools
import math

import jax
import jax.numpy as jnp
from jax import lax
from jax.experimental import pallas as pl
from jax.experimental.pallas import tpu as pltpu
from jax.sharding import PartitionSpec as P

TERMS = 8
REACH = TERMS - 1
LANES = 128
SUBLANES = 8

damping = 0.1

SINE = (0.5, -0.010416666045784950, 6.510379898820e-05, -1.9366727e-07, 3.26248263e-10)


def horner(powers, x):
    total = powers[-1] * x + powers[-2]
    for power in powers[-3::-1]:
        total = total * x + power
    return total


def node_phases(wavenum):
    square = wavenum * wavenum
    absorb = damping * square
    absorb_square = absorb * absorb
    phases = []
    for node in range(TERMS):
        angle = math.pi * (node + 0.5) / TERMS
        excess = square - angle * angle
        modulus_square = excess * excess + absorb_square
        doubled = modulus_square * lax.rsqrt(modulus_square) + jnp.abs(excess)
        inverse = lax.rsqrt(doubled)
        larger = doubled * inverse
        smaller = absorb * inverse
        propagating = excess >= 0
        real_part = jnp.where(propagating, larger, smaller)
        imag_part = jnp.where(propagating, smaller, larger)
        attenuation = jnp.exp2(imag_part * (-math.sqrt(0.5) / math.log(2.0)))
        sine = real_part * horner(SINE, real_part * real_part)
        sine_square = sine * sine
        rest = 2.0 - sine_square
        phase_re = attenuation * (1.0 - sine_square)
        phase_im = attenuation * (sine * (rest * lax.rsqrt(rest)))
        phases.append((phase_re, phase_im))
    return phases


def cosine_sums(values):
    half = TERMS // 2
    both = [values[j] + values[TERMS - 1 - j] for j in range(half)]
    apart = [values[j] - values[TERMS - 1 - j] for j in range(half)]
    outer, inner = both[0] + both[3], both[1] + both[2]
    outer_gap, inner_gap = both[0] - both[3], both[1] - both[2]
    scale = 2.0 / TERMS
    c1, c2, c3 = (scale * math.cos(math.pi * m / 8) for m in (1, 2, 3))
    sums = [None] * TERMS
    sums[0] = (1.0 / TERMS) * (outer + inner)
    sums[4] = c2 * (outer - inner)
    sums[2] = c1 * outer_gap + c3 * inner_gap
    sums[6] = c3 * outer_gap - c1 * inner_gap
    for order in range(1, TERMS, 2):
        row = [scale * math.cos(order * math.pi * (j + 0.5) / TERMS) for j in range(half)]
        sums[order] = (row[0] * apart[0] + row[1] * apart[1]) + (row[2] * apart[2] + row[3] * apart[3])
    return sums


def window(rows, later, two):
    return (0 if two else -REACH * later), rows + REACH * later


def strided(row, tiles):
    return (row // SUBLANES) * SUBLANES * tiles + row % SUBLANES


def either(flip, here, there):
    return here + flip * (there - here)


def spreader(tiles):
    lane = lax.broadcasted_iota(jnp.int32, (tiles, LANES), 1)
    tile = lax.broadcasted_iota(jnp.int32, (tiles, LANES), 0)
    first_lane, last_lane = lane == 0, lane == LANES - 1
    first_tile, last_tile = tile == 0, tile == tiles - 1

    def spread(values):
        left = pltpu.roll(values, 1, 1)
        right = pltpu.roll(values, LANES - 1, 1)
        before = jnp.where(first_tile, 0.0, pltpu.roll(left, 1, 0))
        after = jnp.where(last_tile, 0.0, pltpu.roll(right, tiles - 1, 0))
        left = jnp.where(first_lane, before, left)
        right = jnp.where(last_lane, after, right)
        return (values + values) + (left + right)

    return spread


def chebyshev(levels, fields, low, high, lowest, rows, two):
    spread = spreader(levels.shape[3])
    if not two:
        lat = lax.axis_index("lat")
        inside_low = (lat > 0).astype(jnp.float32)
        inside_high = (lat < lax.axis_size("lat") - 1).astype(jnp.float32)
    for order in range(1, TERMS):
        left = TERMS - 1 - order
        begin, end = (low if two else low - left), high + left
        above = [None if two else spread(levels[order - 1, f, begin - 1 - lowest]) for f in fields]
        here = [spread(levels[order - 1, f, begin - lowest]) for f in fields]
        for row in range(begin, end):
            for k, f in enumerate(fields):
                below = spread(levels[order - 1, f, row + 1 - lowest])
                total = (here[k] + here[k]) + below
                if above[k] is not None:
                    total = total + above[k]
                centre = levels[order - 1, f, row - lowest]
                if order == 1:
                    value = 0.125 * total - centre
                else:
                    value = (0.25 * total - (centre + centre)) - levels[order - 2, f, row - lowest]
                if not two and row < 0:
                    value = value * inside_low
                if not two and row >= rows:
                    value = value * inside_high
                levels[order, f, row - lowest] = value
                above[k], here[k] = here[k], below


def first_kernel(rows, depth_steps, two, conjugate, *refs):
    fields, levels = refs[:-1], refs[-1]
    tiles = levels.shape[3]
    flip = lax.axis_index("lat")
    low, high = window(rows, depth_steps - 1, two)
    lowest = low if two else low - REACH
    for row in range(lowest, high + REACH):
        if two:
            side = 0 if row < rows else 1
            ref, near = fields[side], row - side * rows
            start = either(flip, strided(near, tiles), strided(rows - 1 - near, tiles))
        else:
            side = 1 if row < 0 else 2 if row >= rows else 0
            ref, start = fields[side], strided(row + (0, rows, -rows)[side], tiles)
        for part in range(2):
            value = ref[part, pl.ds(start, tiles, stride=SUBLANES), :]
            levels[0, part, row - lowest] = -value if part and conjugate else value
    chebyshev(levels, (0, 1), low, high, lowest, rows, two)


def coefficient_kernel(shared, tiles, *refs):
    freq_ref, slow_ref, out_ref = refs[0], refs[1], refs[-1]
    count, rows, _ = slow_ref.shape
    slot = 0
    core = lax.axis_index("freq") & 1
    for bit, other in shared:
        change = {-1: core, -2: 1 - core}.get(other, other)
        slot = 2 * slot + (((lax.axis_index("freq") >> bit) & 1) ^ change)
    freq = freq_ref[...]

    def body(piece, carry):
        place = (piece << len(shared)) + slot
        for start in range(0, rows, SUBLANES):
            phases = node_phases(freq * slow_ref[piece, start : start + SUBLANES, :])
            for part in range(2):
                for order, value in enumerate(cosine_sums([p[part] for p in phases])):
                    out_ref[order, part, pl.ds(start * tiles + place, SUBLANES, stride=tiles), :] = value
        return carry

    lax.fori_loop(0, count, body, 0)


def main_kernel(setup, coef_ref, src_levels, rec_levels, *refs):
    rows, halo, depth_steps, two, packed, width = setup
    image_refs, (final_ref, levels) = refs[:-2], refs[-2:]
    tiles = levels.shape[3]
    flip = lax.axis_index("lat")
    lane = lax.broadcasted_iota(jnp.int32, (tiles, LANES), 1)
    tile = lax.broadcasted_iota(jnp.int32, (tiles, LANES), 0)
    in_low = lane < width
    if packed:
        parity, me, count = tile * 0, lax.axis_index("freq"), lax.axis_size("freq")
        for bit in range(count.bit_length() - 1):
            parity = parity ^ (tile >> bit) ^ (me >> bit)
        keeps_even = (parity & 1) == 0

    def own(row):
        return either(flip, row, rows - 1 - row) if two else row

    def own_start(row):
        return either(flip, strided(row, tiles), strided(rows - 1 - row, tiles)) if two else strided(row, tiles)

    def coef_row(step, row):
        sides = 1 if two else 2
        if step:
            return rows + sides * halo + (step - 1) * rows + own(row)
        if 0 <= row < rows:
            return own(row)
        if two:
            return rows + either(flip, row - rows, halo - 1 - (row - rows))
        return rows + halo + (row if row < 0 else row - rows)

    images = []
    for step in range(depth_steps):
        later = depth_steps - 1 - step
        low, high = window(rows, later, two)
        lowest = window(rows, max(later, 1), two)[0]
        if step:

            def pair_fields(pair, carry, low=low, high=high, lowest=lowest):
                chebyshev(levels, (2 * pair, 2 * pair + 1), low, high, lowest, rows, two)
                return carry

            lax.fori_loop(0, 2, pair_fields, 0)
        top = low if two else low - REACH
        next_lowest = window(rows, max(later - 1, 1), two)[0]
        row_images = []
        for row in range(low, high):
            start = pl.multiple_of(coef_row(step, row) * tiles, SUBLANES)
            coefs = [
                [coef_ref[order, part, pl.ds(start, tiles), :] for part in range(2)]
                for order in range(TERMS)
            ]
            outs = []
            for pair in range(2):
                real = imag = None
                for order, (coef_re, coef_im) in enumerate(coefs):
                    if step:
                        field_re = levels[order, 2 * pair, row - lowest]
                        field_im = levels[order, 2 * pair + 1, row - lowest]
                    else:
                        source = rec_levels if pair else src_levels
                        field_re, field_im = source[order, 0, row - top], source[order, 1, row - top]
                    term_re = coef_re * field_re - coef_im * field_im
                    term_im = coef_re * field_im + coef_im * field_re
                    real = term_re if real is None else real + term_re
                    imag = term_im if imag is None else imag + term_im
                outs += [real, imag]
            if later:
                for field in range(4):
                    levels[0, field, row - next_lowest] = outs[field]
            else:
                for field in range(4):
                    final_ref[field, row] = outs[field]
            if not 0 <= row < rows:
                continue
            value = outs[0] * outs[2] - outs[1] * outs[3]
            row_images.append(value)
            if not packed:
                image_refs[0][step, pl.ds(own_start(row), tiles, stride=SUBLANES), :] = value
            elif not later:
                first = images[0][row]
                even = jnp.where(in_low, first, pltpu.roll(value, width, 1))
                odd = jnp.where(in_low, pltpu.roll(first, width, 1), value)
                at = pl.ds(own(row), tiles, stride=rows)
                image_refs[0][at, :] = jnp.where(keeps_even, even, odd)
                image_refs[1][at, :] = jnp.where(keeps_even, odd, even)
        images.append(row_images)


def finish_kernel(two, final_ref, src_ref, rec_ref):
    _, rows, tiles, _ = final_ref.shape
    flip = lax.axis_index("lat")
    for row in range(rows):
        start = strided(row, tiles)
        if two:
            start = either(flip, start, strided(rows - 1 - row, tiles))
        at = pl.ds(start, tiles, stride=SUBLANES)
        src_ref[0, at, :] = final_ref[0, row]
        src_ref[1, at, :] = final_ref[1, row]
        rec_ref[0, at, :] = final_ref[2, row]
        rec_ref[1, at, :] = -final_ref[3, row]


def tiled(block):
    parts, rows, columns = block.shape
    split = block.reshape(parts, rows // SUBLANES, SUBLANES, columns // LANES, LANES)
    return split.transpose(0, 1, 3, 2, 4).reshape(parts, rows * columns // LANES, LANES)


def untiled(block, rows):
    parts, count, _ = block.shape
    tiles = count // rows
    split = block.reshape(parts, rows // SUBLANES, tiles, SUBLANES, LANES)
    return split.transpose(0, 1, 3, 2, 4).reshape(parts, rows, tiles * LANES)


def from_sides(block):
    count = lax.axis_size("lat")
    if count == 2:
        return [lax.ppermute(block, "lat", [(0, 1), (1, 0)])]
    return [
        lax.ppermute(block, "lat", [(i, i - side) for i in range(count) if 0 <= i - side < count]) for side in (-1, 1)
    ]


def partner(block, mask):
    return lax.ppermute(block, "freq", [(i, i ^ mask) for i in range(lax.axis_size("freq"))])


VMEM = pl.BlockSpec(memory_space=pltpu.VMEM)
COST = pl.CostEstimate(flops=1 << 26, bytes_accessed=1 << 22, transcendentals=0)


def call(kernel, shapes, *operands, mib=2, **options):
    single = not isinstance(shapes, list)
    outs = [jax.ShapeDtypeStruct(shape, jnp.float32) for shape in ([shapes] if single else shapes)]
    options.setdefault("in_specs", [VMEM] * len(operands))
    return pl.pallas_call(
        kernel,
        out_shape=outs[0] if single else outs,
        out_specs=VMEM if single else [VMEM] * len(outs),
        compiler_params=pltpu.CompilerParams(vmem_limit_bytes=mib << 20),
        **options,
    )(*operands)


def bundle_kernel(halo, two, *refs):
    layers, sides, out = refs[: -2 if two else -3], refs[-2 if two else -3 : -1], refs[-1]
    rows = layers[0].shape[0]
    out[:rows, :] = layers[0][...]
    if two:
        start = pl.multiple_of(lax.axis_index("lat") * (rows - halo), SUBLANES)
        out[rows : rows + halo, :] = sides[0][0, pl.ds(start, halo), :]
    else:
        out[rows : rows + halo, :] = sides[0][0, rows - halo :, :]
        out[rows + halo : rows + 2 * halo, :] = sides[1][0, :halo, :]
    after = rows + halo * len(sides)
    for step, layer in enumerate(layers[1:]):
        out[after + step * rows : after + (step + 1) * rows, :] = layer[...]


def pair_kernel(halo, *refs):
    layers, (core, out, edge) = refs[:-3], refs[-3:]
    rows = layers[0].shape[0]
    upper = (lax.axis_index("freq") & 1) != 0
    for step, layer in enumerate(layers):
        mine, other = layer[...], core[step]
        pair = jnp.concatenate([jnp.where(upper, other, mine), jnp.where(upper, mine, other)], axis=1)
        out[step * rows : (step + 1) * rows, :] = pair
    start = pl.multiple_of((1 - lax.axis_index("lat")) * (rows - halo), SUBLANES)
    edge[...] = out[pl.ds(start, halo), :]


def tile_kernel(pair, edge, freq, out, freq_out):
    halo, rows = edge.shape[0], out.shape[0] - edge.shape[0]
    first = rows // 2
    out[:first, :] = pair[:first, :]
    out[first : first + halo, :] = edge[...]
    out[first + halo :, :] = pair[first:, :]
    freq_out[...] = freq[...]


def beside_kernel(bit, mine, other, out):
    upper = ((lax.axis_index("freq") >> bit) & 1) != 0
    first, second = mine[...], other[...]
    out[...] = jnp.concatenate([jnp.where(upper, second, first), jnp.where(upper, first, second)], axis=1)


def pick_kernel(first, second, out):
    out[...] = jnp.where((lax.axis_index("freq") & 1) != 0, second[...], first[...])


def stack_kernel(bit, mine, other, out):
    slot = (lax.axis_index("freq") >> bit) & 1
    for piece in range(mine.shape[0]):
        out[2 * piece + slot] = mine[piece]
        out[2 * piece + 1 - slot] = other[piece]


def gather_columns(block, done=0):
    count = lax.axis_size("freq")
    rows, width = block.shape
    width >>= done
    bits = range(count.bit_length() - 1)
    inner = [b for b in bits if width << b < LANES]
    outer = [b for b in bits if width << b >= LANES][::-1]
    for b in inner[done:]:
        other = partner(block, 1 << b)
        shape = (rows, 2 * block.shape[1])
        block = call(functools.partial(beside_kernel, b), shape, block, other, cost_estimate=COST)
    block = block[None]
    cross = 1 if inner else 0
    for b in outer[:-2]:
        other = partner(block, (1 << b) | cross)
        shape = (2 * block.shape[0], *block.shape[1:])
        block = call(functools.partial(stack_kernel, b), shape, block, other, cost_estimate=COST)
    high, low = outer[-2:]
    other = partner(block, (1 << high) | cross)
    mine = [(block, ((high, 0), (low, 0))), (other, ((high, 1), (low, 0)))]
    if not cross:
        theirs = [partner(part, 1 << low) for part in (block, other)]
        return mine + [(theirs[0], ((high, 0), (low, 1))), (theirs[1], ((high, 1), (low, 1)))]
    piece = call(pick_kernel, block.shape, block, other, cost_estimate=COST)
    near = partner(piece, (1 << low) | 1)
    far = partner(near, 1)
    return mine + [(near, ((high, -2), (low, 1))), (far, ((high, -1), (low, 1)))]


def halve_kernel(bit, held, came, keep, send):
    slot = (lax.axis_index("freq") >> bit) & 1
    for piece in range(keep.shape[0]):
        here, there = 2 * piece + slot, 2 * piece + 1 - slot
        send[piece] = held[there] + came[there]
        keep[piece] = held[here] + came[here]


def last_kernel(scale, held, came, out):
    total = (held[0] + came[0]) * scale
    width = out.shape[2]
    for step in range(out.shape[0]):
        out[step] = total[:, step * width : (step + 1) * width]


def scatter_sum(keep, send, rows, scale, out_shape):
    count = lax.axis_size("freq")
    pieces = count // 2
    held = keep.reshape(pieces, rows, LANES)
    came = partner(send, 1).reshape(pieces, rows, LANES)
    for b in range(1, count.bit_length() - 1):
        pieces //= 2
        shapes = [(pieces, rows, LANES)] * 2
        held, send = call(functools.partial(halve_kernel, b), shapes, held, came)
        came = partner(send, (1 << b) | 1)
    return call(functools.partial(last_kernel, scale), out_shape, held, came)


def shards(frequencies, slowness, src_field, rec_field):
    depth_steps, rows, width = slowness.shape
    tiles = src_field.shape[3] // LANES
    freq_count = lax.axis_size("freq")
    two = lax.axis_size("lat") == 2
    packed = depth_steps == 2 and width * depth_steps == LANES
    norm_factor = 1.0 / math.sqrt(frequencies.shape[0] * freq_count)
    halo = -(-REACH * (depth_steps - 1) // SUBLANES) * SUBLANES
    low, high = window(rows, depth_steps - 1, two)
    span = high + REACH - (low if two else low - REACH)
    later_span = window(rows, 1, two)[1] - window(rows, 1, two)[0]

    src_sides = from_sides(src_field)
    rec_sides = from_sides(rec_field)
    coef_rows = depth_steps * rows + halo * len(src_sides)
    layers = [slowness[z] for z in range(depth_steps)]
    freq = jnp.broadcast_to(frequencies, (SUBLANES, LANES))
    if two and 2 * width == LANES and depth_steps == 2:
        core = partner(slowness, 1)
        shapes = [(depth_steps * rows, LANES), (halo, LANES)]
        pair, edge = call(functools.partial(pair_kernel, halo), shapes, *layers, core, cost_estimate=COST)
        (edge,) = from_sides(edge)
        shapes = [(coef_rows, LANES), (SUBLANES, LANES)]
        block, freq = call(tile_kernel, shapes, pair, edge, freq, cost_estimate=COST)
        parts = gather_columns(block, done=1)
    else:
        slow_sides = from_sides(slowness)
        kernel = functools.partial(bundle_kernel, halo, two)
        bundle = call(kernel, (coef_rows, width), *layers, *slow_sides)
        parts = gather_columns(bundle)

    def first_levels(own, sides, conjugate):
        fields = [tiled(x[0]) for x in (own, *sides)]
        kernel = functools.partial(first_kernel, rows, depth_steps, two, conjugate)
        return call(kernel, (TERMS, 2, span, tiles, LANES), *fields, mib=4, cost_estimate=COST)

    src_levels = first_levels(src_field, src_sides, False)
    rec_levels = first_levels(rec_field, rec_sides, True)

    coef_shape = (TERMS, 2, coef_rows * tiles, LANES)
    coefs = []
    for part, shared in parts:
        coefs = [
            call(
                functools.partial(coefficient_kernel, shared, tiles),
                coef_shape,
                freq,
                part,
                *coefs,
                mib=8,
                input_output_aliases={2: 0} if coefs else {},
                cost_estimate=COST,
            )
        ]

    image_shape = (tiles * rows, LANES) if packed else (depth_steps, rows * tiles, LANES)
    field_shape = (2, rows * tiles, LANES)
    image_shapes = [image_shape] * (2 if packed else 1)
    setup = (rows, halo, depth_steps, two, packed, width)
    *image, final = call(
        functools.partial(main_kernel, setup),
        [*image_shapes, (4, rows, tiles, LANES)],
        coefs[0],
        src_levels,
        rec_levels,
        mib=16,
        scratch_shapes=[pltpu.VMEM((TERMS, 4, later_span, tiles, LANES), jnp.float32)],
    )

    src, rec = call(functools.partial(finish_kernel, two), [field_shape] * 2, final, mib=4, cost_estimate=COST)

    if packed:
        depth_image = scatter_sum(*image, rows, norm_factor, (depth_steps, rows, width))
    else:
        whole = untiled(image[0], rows).reshape(depth_steps, rows, freq_count, width)
        pieces = whole.transpose(2, 0, 1, 3)
        depth_image = jnp.sum(lax.all_to_all(pieces, "freq", 0, 0, tiled=True), axis=0) * norm_factor
    return (depth_image, untiled(src, rows)[None], untiled(rec, rows)[None])


def solution(mesh):
    placed = (
        P("freq"),
        P(None, "lat", "freq"),
        P("freq", None, "lat", None),
        P("freq", None, "lat", None),
    )
    return jax.shard_map(
        shards,
        mesh=mesh,
        in_specs=placed,
        out_specs=(
            P(None, "lat", "freq"),
            P("freq", None, "lat", None),
            P("freq", None, "lat", None),
        ),
        check_vma=False,
    )
```

```python
import functools
import math

import jax
import jax.numpy as jnp
from jax import lax
from jax.experimental import pallas as pl
from jax.experimental.pallas import tpu as pltpu
from jax.sharding import PartitionSpec as P

TERMS = 8
REACH = TERMS - 1
LANES = 128
SUBLANES = 8

damping = 0.1

SINE = (0.5, -0.010416666045784950, 6.510379898820e-05, -1.9366727e-07, 3.26248263e-10)


def horner(powers, x):
    total = powers[-1] * x + powers[-2]
    for power in powers[-3::-1]:
        total = total * x + power
    return total


def node_phases(wavenum):
    square = wavenum * wavenum
    absorb = damping * square
    absorb_square = absorb * absorb
    phases = []
    for node in range(TERMS):
        angle = math.pi * (node + 0.5) / TERMS
        excess = square - angle * angle
        modulus_square = excess * excess + absorb_square
        doubled = modulus_square * lax.rsqrt(modulus_square) + jnp.abs(excess)
        inverse = lax.rsqrt(doubled)
        larger = doubled * inverse
        smaller = absorb * inverse
        propagating = excess >= 0
        real_part = jnp.where(propagating, larger, smaller)
        imag_part = jnp.where(propagating, smaller, larger)
        attenuation = jnp.exp2(imag_part * (-math.sqrt(0.5) / math.log(2.0)))
        sine = real_part * horner(SINE, real_part * real_part)
        sine_square = sine * sine
        rest = 2.0 - sine_square
        phase_re = attenuation * (1.0 - sine_square)
        phase_im = attenuation * (sine * (rest * lax.rsqrt(rest)))
        phases.append((phase_re, phase_im))
    return phases


def cosine_sums(values):
    half = TERMS // 2
    both = [values[j] + values[TERMS - 1 - j] for j in range(half)]
    apart = [values[j] - values[TERMS - 1 - j] for j in range(half)]
    outer, inner = both[0] + both[3], both[1] + both[2]
    outer_gap, inner_gap = both[0] - both[3], both[1] - both[2]
    scale = 2.0 / TERMS
    c1, c2, c3 = (scale * math.cos(math.pi * m / 8) for m in (1, 2, 3))
    sums = [None] * TERMS
    sums[0] = (1.0 / TERMS) * (outer + inner)
    sums[4] = c2 * (outer - inner)
    sums[2] = c1 * outer_gap + c3 * inner_gap
    sums[6] = c3 * outer_gap - c1 * inner_gap
    for order in range(1, TERMS, 2):
        row = [scale * math.cos(order * math.pi * (j + 0.5) / TERMS) for j in range(half)]
        sums[order] = (row[0] * apart[0] + row[1] * apart[1]) + (row[2] * apart[2] + row[3] * apart[3])
    return sums


def window(rows, later, two):
    return (0 if two else -REACH * later), rows + REACH * later


def strided(row, tiles):
    return (row // SUBLANES) * SUBLANES * tiles + row % SUBLANES


def either(flip, here, there):
    return here + flip * (there - here)


def spreader(tiles):
    lane = lax.broadcasted_iota(jnp.int32, (tiles, LANES), 1)
    tile = lax.broadcasted_iota(jnp.int32, (tiles, LANES), 0)
    first_lane, last_lane = lane == 0, lane == LANES - 1
    first_tile, last_tile = tile == 0, tile == tiles - 1

    def spread(values):
        left = pltpu.roll(values, 1, 1)
        right = pltpu.roll(values, LANES - 1, 1)
        before = jnp.where(first_tile, 0.0, pltpu.roll(left, 1, 0))
        after = jnp.where(last_tile, 0.0, pltpu.roll(right, tiles - 1, 0))
        left = jnp.where(first_lane, before, left)
        right = jnp.where(last_lane, after, right)
        return (values + values) + (left + right)

    return spread


def chebyshev(levels, fields, low, high, lowest, rows, two):
    spread = spreader(levels.shape[3])
    if not two:
        lat = lax.axis_index("lat")
        inside_low = (lat > 0).astype(jnp.float32)
        inside_high = (lat < lax.axis_size("lat") - 1).astype(jnp.float32)
    for order in range(1, TERMS):
        left = TERMS - 1 - order
        begin, end = (low if two else low - left), high + left
        above = [None if two else levels[order - 1, f, begin - 1 - lowest] for f in fields]
        here = [levels[order - 1, f, begin - lowest] for f in fields]
        for row in range(begin, end):
            for k, f in enumerate(fields):
                below = levels[order - 1, f, row + 1 - lowest]
                centre = here[k]
                total = (centre + centre) + below
                if above[k] is not None:
                    total = total + above[k]
                total = spread(total)
                if order == 1:
                    value = 0.125 * total - centre
                else:
                    value = (0.25 * total - (centre + centre)) - levels[order - 2, f, row - lowest]
                if not two and row < 0:
                    value = value * inside_low
                if not two and row >= rows:
                    value = value * inside_high
                levels[order, f, row - lowest] = value
                above[k], here[k] = here[k], below


def first_kernel(rows, depth_steps, two, conjugate, *refs):
    fields, levels = refs[:-1], refs[-1]
    tiles = levels.shape[3]
    flip = lax.axis_index("lat")
    low, high = window(rows, depth_steps - 1, two)
    lowest = low if two else low - REACH
    for row in range(lowest, high + REACH):
        if two:
            side = 0 if row < rows else 1
            ref, near = fields[side], row - side * rows
            start = either(flip, strided(near, tiles), strided(rows - 1 - near, tiles))
        else:
            side = 1 if row < 0 else 2 if row >= rows else 0
            ref, start = fields[side], strided(row + (0, rows, -rows)[side], tiles)
        for part in range(2):
            value = ref[part, pl.ds(start, tiles, stride=SUBLANES), :]
            levels[0, part, row - lowest] = -value if part and conjugate else value
    chebyshev(levels, (0, 1), low, high, lowest, rows, two)


def coefficient_kernel(shared, tiles, *refs):
    freq_ref, slow_ref, out_ref = refs[0], refs[1], refs[-1]
    count, rows, _ = slow_ref.shape
    slot = 0
    core = lax.axis_index("freq") & 1
    for bit, other in shared:
        change = {-1: core, -2: 1 - core}.get(other, other)
        slot = 2 * slot + (((lax.axis_index("freq") >> bit) & 1) ^ change)
    freq = freq_ref[...]

    def body(piece, carry):
        place = (piece << len(shared)) + slot
        for start in range(0, rows, SUBLANES):
            phases = node_phases(freq * slow_ref[piece, start : start + SUBLANES, :])
            for part in range(2):
                for order, value in enumerate(cosine_sums([p[part] for p in phases])):
                    out_ref[order, part, pl.ds(start * tiles + place, SUBLANES, stride=tiles), :] = value
        return carry

    lax.fori_loop(0, count, body, 0)


def main_kernel(setup, coef_ref, src_levels, rec_levels, *refs):
    rows, halo, depth_steps, two, packed, width = setup
    image_refs, (final_ref, levels) = refs[:-2], refs[-2:]
    tiles = levels.shape[3]
    flip = lax.axis_index("lat")
    lane = lax.broadcasted_iota(jnp.int32, (tiles, LANES), 1)
    tile = lax.broadcasted_iota(jnp.int32, (tiles, LANES), 0)
    in_low = lane < width
    if packed:
        parity, me, count = tile * 0, lax.axis_index("freq"), lax.axis_size("freq")
        for bit in range(count.bit_length() - 1):
            parity = parity ^ (tile >> bit) ^ (me >> bit)
        keeps_even = (parity & 1) == 0

    def own(row):
        return either(flip, row, rows - 1 - row) if two else row

    def own_start(row):
        return either(flip, strided(row, tiles), strided(rows - 1 - row, tiles)) if two else strided(row, tiles)

    def coef_row(step, row):
        sides = 1 if two else 2
        if step:
            return rows + sides * halo + (step - 1) * rows + own(row)
        if 0 <= row < rows:
            return own(row)
        if two:
            return rows + either(flip, row - rows, halo - 1 - (row - rows))
        return rows + halo + (row if row < 0 else row - rows)

    images = []
    for step in range(depth_steps):
        later = depth_steps - 1 - step
        low, high = window(rows, later, two)
        lowest = window(rows, max(later, 1), two)[0]
        if step:

            def pair_fields(pair, carry, low=low, high=high, lowest=lowest):
                chebyshev(levels, (2 * pair, 2 * pair + 1), low, high, lowest, rows, two)
                return carry

            lax.fori_loop(0, 2, pair_fields, 0)
        top = low if two else low - REACH
        next_lowest = window(rows, max(later - 1, 1), two)[0]
        row_images = []
        for row in range(low, high):
            start = pl.multiple_of(coef_row(step, row) * tiles, SUBLANES)
            coefs = [
                [coef_ref[order, part, pl.ds(start, tiles), :] for part in range(2)]
                for order in range(TERMS)
            ]
            outs = []
            for pair in range(2):
                real = imag = None
                for order, (coef_re, coef_im) in enumerate(coefs):
                    if step:
                        field_re = levels[order, 2 * pair, row - lowest]
                        field_im = levels[order, 2 * pair + 1, row - lowest]
                    else:
                        source = rec_levels if pair else src_levels
                        field_re, field_im = source[order, 0, row - top], source[order, 1, row - top]
                    term_re = coef_re * field_re - coef_im * field_im
                    term_im = coef_re * field_im + coef_im * field_re
                    real = term_re if real is None else real + term_re
                    imag = term_im if imag is None else imag + term_im
                outs += [real, imag]
            if later:
                for field in range(4):
                    levels[0, field, row - next_lowest] = outs[field]
            else:
                for field in range(4):
                    final_ref[field, row] = outs[field]
            if not 0 <= row < rows:
                continue
            value = outs[0] * outs[2] - outs[1] * outs[3]
            row_images.append(value)
            if not packed:
                image_refs[0][step, pl.ds(own_start(row), tiles, stride=SUBLANES), :] = value
            elif not later:
                first = images[0][row]
                even = jnp.where(in_low, first, pltpu.roll(value, width, 1))
                odd = jnp.where(in_low, pltpu.roll(first, width, 1), value)
                at = pl.ds(own(row), tiles, stride=rows)
                image_refs[0][at, :] = jnp.where(keeps_even, even, odd)
                image_refs[1][at, :] = jnp.where(keeps_even, odd, even)
        images.append(row_images)


def finish_kernel(two, final_ref, src_ref, rec_ref):
    _, rows, tiles, _ = final_ref.shape
    flip = lax.axis_index("lat")
    for row in range(rows):
        start = strided(row, tiles)
        if two:
            start = either(flip, start, strided(rows - 1 - row, tiles))
        at = pl.ds(start, tiles, stride=SUBLANES)
        src_ref[0, at, :] = final_ref[0, row]
        src_ref[1, at, :] = final_ref[1, row]
        rec_ref[0, at, :] = final_ref[2, row]
        rec_ref[1, at, :] = -final_ref[3, row]


def tiled(block):
    parts, rows, columns = block.shape
    split = block.reshape(parts, rows // SUBLANES, SUBLANES, columns // LANES, LANES)
    return split.transpose(0, 1, 3, 2, 4).reshape(parts, rows * columns // LANES, LANES)


def untiled(block, rows):
    parts, count, _ = block.shape
    tiles = count // rows
    split = block.reshape(parts, rows // SUBLANES, tiles, SUBLANES, LANES)
    return split.transpose(0, 1, 3, 2, 4).reshape(parts, rows, tiles * LANES)


def from_sides(block):
    count = lax.axis_size("lat")
    if count == 2:
        return [lax.ppermute(block, "lat", [(0, 1), (1, 0)])]
    return [
        lax.ppermute(block, "lat", [(i, i - side) for i in range(count) if 0 <= i - side < count]) for side in (-1, 1)
    ]


def partner(block, mask):
    return lax.ppermute(block, "freq", [(i, i ^ mask) for i in range(lax.axis_size("freq"))])


VMEM = pl.BlockSpec(memory_space=pltpu.VMEM)
COST = pl.CostEstimate(flops=1 << 26, bytes_accessed=1 << 22, transcendentals=0)


def call(kernel, shapes, *operands, mib=2, **options):
    single = not isinstance(shapes, list)
    outs = [jax.ShapeDtypeStruct(shape, jnp.float32) for shape in ([shapes] if single else shapes)]
    options.setdefault("in_specs", [VMEM] * len(operands))
    return pl.pallas_call(
        kernel,
        out_shape=outs[0] if single else outs,
        out_specs=VMEM if single else [VMEM] * len(outs),
        compiler_params=pltpu.CompilerParams(vmem_limit_bytes=mib << 20),
        **options,
    )(*operands)


def bundle_kernel(halo, two, *refs):
    layers, sides, out = refs[: -2 if two else -3], refs[-2 if two else -3 : -1], refs[-1]
    rows = layers[0].shape[0]
    out[:rows, :] = layers[0][...]
    if two:
        start = pl.multiple_of(lax.axis_index("lat") * (rows - halo), SUBLANES)
        out[rows : rows + halo, :] = sides[0][0, pl.ds(start, halo), :]
    else:
        out[rows : rows + halo, :] = sides[0][0, rows - halo :, :]
        out[rows + halo : rows + 2 * halo, :] = sides[1][0, :halo, :]
    after = rows + halo * len(sides)
    for step, layer in enumerate(layers[1:]):
        out[after + step * rows : after + (step + 1) * rows, :] = layer[...]


def pair_kernel(halo, *refs):
    layers, (core, out, edge) = refs[:-3], refs[-3:]
    rows = layers[0].shape[0]
    upper = (lax.axis_index("freq") & 1) != 0
    for step, layer in enumerate(layers):
        mine, other = layer[...], core[step]
        pair = jnp.concatenate([jnp.where(upper, other, mine), jnp.where(upper, mine, other)], axis=1)
        out[step * rows : (step + 1) * rows, :] = pair
    start = pl.multiple_of((1 - lax.axis_index("lat")) * (rows - halo), SUBLANES)
    edge[...] = out[pl.ds(start, halo), :]


def tile_kernel(pair, edge, freq, out, freq_out):
    halo, rows = edge.shape[0], out.shape[0] - edge.shape[0]
    first = rows // 2
    out[:first, :] = pair[:first, :]
    out[first : first + halo, :] = edge[...]
    out[first + halo :, :] = pair[first:, :]
    freq_out[...] = freq[...]


def beside_kernel(bit, mine, other, out):
    upper = ((lax.axis_index("freq") >> bit) & 1) != 0
    first, second = mine[...], other[...]
    out[...] = jnp.concatenate([jnp.where(upper, second, first), jnp.where(upper, first, second)], axis=1)


def pick_kernel(first, second, out):
    out[...] = jnp.where((lax.axis_index("freq") & 1) != 0, second[...], first[...])


def stack_kernel(bit, mine, other, out):
    slot = (lax.axis_index("freq") >> bit) & 1
    for piece in range(mine.shape[0]):
        out[2 * piece + slot] = mine[piece]
        out[2 * piece + 1 - slot] = other[piece]


def gather_columns(block, done=0):
    count = lax.axis_size("freq")
    rows, width = block.shape
    width >>= done
    bits = range(count.bit_length() - 1)
    inner = [b for b in bits if width << b < LANES]
    outer = [b for b in bits if width << b >= LANES][::-1]
    for b in inner[done:]:
        other = partner(block, 1 << b)
        shape = (rows, 2 * block.shape[1])
        block = call(functools.partial(beside_kernel, b), shape, block, other, cost_estimate=COST)
    block = block[None]
    cross = 1 if inner else 0
    for b in outer[:-2]:
        other = partner(block, (1 << b) | cross)
        shape = (2 * block.shape[0], *block.shape[1:])
        block = call(functools.partial(stack_kernel, b), shape, block, other, cost_estimate=COST)
    high, low = outer[-2:]
    other = partner(block, (1 << high) | cross)
    mine = [(block, ((high, 0), (low, 0))), (other, ((high, 1), (low, 0)))]
    if not cross:
        theirs = [partner(part, 1 << low) for part in (block, other)]
        return mine + [(theirs[0], ((high, 0), (low, 1))), (theirs[1], ((high, 1), (low, 1)))]
    piece = call(pick_kernel, block.shape, block, other, cost_estimate=COST)
    near = partner(piece, (1 << low) | 1)
    far = partner(near, 1)
    return mine + [(near, ((high, -2), (low, 1))), (far, ((high, -1), (low, 1)))]


def halve_kernel(bit, held, came, keep, send):
    slot = (lax.axis_index("freq") >> bit) & 1
    for piece in range(keep.shape[0]):
        here, there = 2 * piece + slot, 2 * piece + 1 - slot
        send[piece] = held[there] + came[there]
        keep[piece] = held[here] + came[here]


def last_kernel(scale, held, came, out):
    total = (held[0] + came[0]) * scale
    width = out.shape[2]
    for step in range(out.shape[0]):
        out[step] = total[:, step * width : (step + 1) * width]


def scatter_sum(keep, send, rows, scale, out_shape):
    count = lax.axis_size("freq")
    pieces = count // 2
    held = keep.reshape(pieces, rows, LANES)
    came = partner(send, 1).reshape(pieces, rows, LANES)
    for b in range(1, count.bit_length() - 1):
        pieces //= 2
        shapes = [(pieces, rows, LANES)] * 2
        held, send = call(functools.partial(halve_kernel, b), shapes, held, came)
        came = partner(send, (1 << b) | 1)
    return call(functools.partial(last_kernel, scale), out_shape, held, came)


def shards(frequencies, slowness, src_field, rec_field):
    depth_steps, rows, width = slowness.shape
    tiles = src_field.shape[3] // LANES
    freq_count = lax.axis_size("freq")
    two = lax.axis_size("lat") == 2
    packed = depth_steps == 2 and width * depth_steps == LANES
    norm_factor = 1.0 / math.sqrt(frequencies.shape[0] * freq_count)
    halo = -(-REACH * (depth_steps - 1) // SUBLANES) * SUBLANES
    low, high = window(rows, depth_steps - 1, two)
    span = high + REACH - (low if two else low - REACH)
    later_span = window(rows, 1, two)[1] - window(rows, 1, two)[0]

    src_sides = from_sides(src_field)
    rec_sides = from_sides(rec_field)
    coef_rows = depth_steps * rows + halo * len(src_sides)
    layers = [slowness[z] for z in range(depth_steps)]
    freq = jnp.broadcast_to(frequencies, (SUBLANES, LANES))
    if two and 2 * width == LANES and depth_steps == 2:
        core = partner(slowness, 1)
        shapes = [(depth_steps * rows, LANES), (halo, LANES)]
        pair, edge = call(functools.partial(pair_kernel, halo), shapes, *layers, core, cost_estimate=COST)
        (edge,) = from_sides(edge)
        shapes = [(coef_rows, LANES), (SUBLANES, LANES)]
        block, freq = call(tile_kernel, shapes, pair, edge, freq, cost_estimate=COST)
        parts = gather_columns(block, done=1)
    else:
        slow_sides = from_sides(slowness)
        kernel = functools.partial(bundle_kernel, halo, two)
        bundle = call(kernel, (coef_rows, width), *layers, *slow_sides)
        parts = gather_columns(bundle)

    def first_levels(own, sides, conjugate):
        fields = [tiled(x[0]) for x in (own, *sides)]
        kernel = functools.partial(first_kernel, rows, depth_steps, two, conjugate)
        return call(kernel, (TERMS, 2, span, tiles, LANES), *fields, mib=4, cost_estimate=COST)

    src_levels = first_levels(src_field, src_sides, False)
    rec_levels = first_levels(rec_field, rec_sides, True)

    coef_shape = (TERMS, 2, coef_rows * tiles, LANES)
    coefs = []
    for part, shared in parts:
        coefs = [
            call(
                functools.partial(coefficient_kernel, shared, tiles),
                coef_shape,
                freq,
                part,
                *coefs,
                mib=8,
                input_output_aliases={2: 0} if coefs else {},
                cost_estimate=COST,
            )
        ]

    image_shape = (tiles * rows, LANES) if packed else (depth_steps, rows * tiles, LANES)
    field_shape = (2, rows * tiles, LANES)
    image_shapes = [image_shape] * (2 if packed else 1)
    setup = (rows, halo, depth_steps, two, packed, width)
    *image, final = call(
        functools.partial(main_kernel, setup),
        [*image_shapes, (4, rows, tiles, LANES)],
        coefs[0],
        src_levels,
        rec_levels,
        mib=16,
        scratch_shapes=[pltpu.VMEM((TERMS, 4, later_span, tiles, LANES), jnp.float32)],
    )

    src, rec = call(functools.partial(finish_kernel, two), [field_shape] * 2, final, mib=4, cost_estimate=COST)

    if packed:
        depth_image = scatter_sum(*image, rows, norm_factor, (depth_steps, rows, width))
    else:
        whole = untiled(image[0], rows).reshape(depth_steps, rows, freq_count, width)
        pieces = whole.transpose(2, 0, 1, 3)
        depth_image = jnp.sum(lax.all_to_all(pieces, "freq", 0, 0, tiled=True), axis=0) * norm_factor
    return (depth_image, untiled(src, rows)[None], untiled(rec, rows)[None])


def solution(mesh):
    placed = (
        P("freq"),
        P(None, "lat", "freq"),
        P("freq", None, "lat", None),
        P("freq", None, "lat", None),
    )
    return jax.shard_map(
        shards,
        mesh=mesh,
        in_specs=placed,
        out_specs=(
            P(None, "lat", "freq"),
            P("freq", None, "lat", None),
            P("freq", None, "lat", None),
        ),
        check_vma=False,
    )
```
